128 devices in a mesh: wide: 16 (over x_lo, y, core), narrow: 8 (over x_hi, z).
Axes of the slice: x: 4 (x_hi: 2, x_lo: 2; x = x_hi * 2 + x_lo), y: 4, z: 4, core: 2. Of those that a mesh axis runs over, the one named last changes fastest.
Arguments:
- inputs: bfloat16 [1792, 16384], P('wide', 'narrow'), may hold values from -6 to 6
- grad_out: bfloat16 [1792, 53248], P('narrow', 'wide'), may hold values from -6 to 6
- w_base: bfloat16 [16384, 53248], P('narrow', 'wide'), may hold values from -0.046875 to 0.046875
- adapter_down_matrix: bfloat16 [16384, 256], P('narrow'), may hold values from -0.046875 to 0.046875
- b_factor: bfloat16 [256, 53248], P(None, 'wide'), may hold values from -0.375 to 0.375
Outputs:
- input_gradient: bfloat16 [1792, 16384], P('wide', 'narrow')
- grad_a: float32 [16384, 256], P('narrow')
- grad_b: float32 [256, 53248], P(None, 'wide')
The draws below stay inside these ranges and needn't reach their ends.
All inputs are finite; a program needn't handle non-finite values.
Results may differ from the reference program's by a relative error of at most 0.0046.
Values may be sent and summed in bfloat16 or wider, within the bound.
A program may use at most 128 MiB of HBM per device.

```python
import jax
import jax.numpy as jnp

D = 16384
F = 53248
R = 256
TOKEN_COUNT = 1792


def spiked(values, key, source, target, shards_of, factor):
    def block_of(axis_at):
        return (jnp.arange(values.shape[axis_at]) // (values.shape[axis_at] // shards_of)).reshape((-1,) + (1,) * (values.ndim - 1 - axis_at))

    first = jax.random.permutation(key, shards_of)[block_of(target)]
    other_side = (block_of(target) + shards_of // 2) % shards_of
    return jnp.where((block_of(source) == first) | (block_of(source) == other_side), factor * values, values)


def levels(key, dims, pieces, least, largest):
    factor_of, own = 1.0, jax.random.fold_in(key, 6)
    for dim, shards_of in pieces:
        draws = jnp.exp(jax.random.uniform(jax.random.fold_in(own, dim), (shards_of,), jnp.float32, least / len(pieces), largest / len(pieces)))
        factor_of = factor_of * jnp.repeat(draws, dims[dim] // shards_of).reshape([-1 if axis == dim else 1 for axis in range(len(dims))])
    return factor_of


def noise(key, shape, scale, bound, split=(), kind=jnp.bfloat16):
    values = jax.random.normal(key, shape, jnp.float32) * scale
    if len(split) > 0:
        values = levels(key, shape, split, -0.22, 0.18) * values
    return jnp.clip(values, min=-bound, max=bound).astype(kind)


def bell_draw_with(stream_key, extent, deviation, limit, split, heavy, dtype=jnp.bfloat16):
    entries = deviation * jax.random.normal(stream_key, extent, jnp.float32)
    if split:
        entries = entries * levels(stream_key, extent, split, -0.22, 0.18)
    return jnp.clip(spiked(entries, jax.random.fold_in(stream_key, 3), *heavy), -limit, limit).astype(dtype)


def setup_inputs(seed: int = 0) -> dict:
    key_list = jax.random.split(jax.random.key(seed), 6)
    inputs = noise(key_list[0], (TOKEN_COUNT, D), 1.0, 6.0, ((0, 16), (1, 8)))
    grad_out = bell_draw_with(key_list[1], (TOKEN_COUNT, F), 1.0, 6.0, ((0, 8), (1, 16)), (1, 0, 16, 2.0))
    w_base = noise(key_list[2], (D, F), D ** -0.5, 0.046875, ((0, 8), (1, 16)))
    adapter_down_matrix = noise(key_list[3], (D, R), D ** -0.5, 0.046875, ((0, 8),))
    b_factor = noise(key_list[4], (R, F), R ** -0.5, 0.375, ((1, 16),))
    return dict(inputs=inputs, grad_out=grad_out, w_base=w_base, adapter_down_matrix=adapter_down_matrix, b_factor=b_factor)


adapter_scale = 2.0


def reference(inputs, grad_out, w_base, adapter_down_matrix, b_factor):
    frozen_input_gradient = jnp.dot(grad_out, w_base.T, preferred_element_type=jnp.float32)
    low_rank_gradient = jnp.dot(grad_out, b_factor.T, preferred_element_type=jnp.float32).astype(jnp.bfloat16)
    input_gradient = (frozen_input_gradient + adapter_scale * jnp.dot(low_rank_gradient, adapter_down_matrix.T, preferred_element_type=jnp.float32)).astype(jnp.bfloat16)
    adapter_matrix = adapter_scale / TOKEN_COUNT
    grad_a = adapter_matrix * jnp.dot(inputs.T, low_rank_gradient, preferred_element_type=jnp.float32)
    low_act = jnp.dot(inputs, adapter_down_matrix, preferred_element_type=jnp.float32).astype(jnp.bfloat16)
    grad_b = adapter_matrix * jnp.dot(low_act.T, grad_out, preferred_element_type=jnp.float32)
    return input_gradient, grad_a, grad_b
```

```python
import jax
import jax.numpy as jnp
from jax import lax
from jax.experimental import pallas as pl
from jax.experimental.pallas import tpu as pltpu
from jax.sharding import PartitionSpec as P

ADAPTER_SCALE = 2.0
ROWS = 112
F_LOCAL = 3328
D_LOCAL = 2048
R = 256
TILE = 256
TILES = (R + D_LOCAL) // TILE
PARTS = 3
PER_PART = TILES // PARTS
STEPS = 8
MESH = pl.DeviceIdType.MESH
BF16 = jnp.bfloat16
F32 = jnp.float32

ORDER = (
    ((0, 0), (0, 1), (1, 0), (0, 3), (1, 1), (0, 2), (1, 2), (1, 3)),
    ((0, 0), (0, 3), (0, 1), (0, 2), (1, 3), (1, 0), (1, 2), (1, 1)),
)


def dot_nt(a, b):
    return lax.dot_general(a, b, (((1,), (1,)), ((), ())), preferred_element_type=F32)


def dot_nn(a, b):
    return lax.dot_general(a, b, (((1,), (0,)), ((), ())), preferred_element_type=F32)


def pick(index, values):
    if isinstance(index, int):
        return values[index]
    out = index * 0 + values[0]
    for i, value in enumerate(values[1:], 1):
        out = out + (index == i).astype(jnp.int32) * (value - values[0])
    return out


def kernel(
    x_hbm, g_hbm, w_hbm, a_hbm, b_hbm,
    ig_ref, ga_ref, gb_ref,
    g, w, a, xs_all, part_send, part_recv, mine, y_recv, y_own, x_send, x_recv,
    lp, l1, l2s, l2r, lo, la, la_t, lg, lg_t,
    ld_sem, g_ss, g_rs, c_ss, c_rs, y_ss, y_rs, x_ss, x_rs,
    in_ss, in_rs, la_ss, la_rs, lg_ss, lg_rs, l1_ss, l1_rs, l2_ss, l2_rs, l3_ss, l3_rs,
):
    wi = lax.axis_index("wide")
    ni = lax.axis_index("narrow")
    xl, y, c = wi // 8, (wi // 2) % 4, wi % 2
    xh, z = ni // 4, ni % 4

    def wide_id(xl_, y_, c_):
        return (xl_ * 4 + y_) * 2 + c_

    def ring(v, k):
        return (v + k) % 4

    def wide_dev(xl_, y_, c_):
        return (wide_id(xl_, y_, c_), ni)

    partner = wide_dev(xl, y, 1 - c)
    x_pair = wide_dev(1 - xl, y, c)
    x_cross = (wi, (1 - xh) * 4 + z)
    z_next = (wi, xh * 4 + ring(z, 1))
    z_prev = (wi, xh * 4 + ring(z, 3))

    def send(src, dst, ss, rs, dev):
        cp = pltpu.make_async_remote_copy(
            src_ref=src, dst_ref=dst, send_sem=ss, recv_sem=rs, device_id=dev, device_id_type=MESH
        )
        cp.start()
        return cp

    def arrived(dst, rs, ss):
        pltpu.make_async_remote_copy(
            src_ref=dst, dst_ref=dst, send_sem=ss, recv_sem=rs, device_id=partner, device_id_type=MESH
        ).wait_recv()

    def sent(src, ss, rs):
        pltpu.make_async_remote_copy(
            src_ref=src, dst_ref=src, send_sem=ss, recv_sem=rs, device_id=partner, device_id_type=MESH
        ).wait_send()

    loads = [
        pltpu.make_async_copy(x_hbm, xs_all.at[wi], ld_sem.at[0]),
        pltpu.make_async_copy(a_hbm, a, ld_sem.at[1]),
        pltpu.make_async_copy(g_hbm.at[pl.ds(0, ROWS)], g.at[0], ld_sem.at[2]),
        pltpu.make_async_copy(g_hbm.at[pl.ds(ROWS, ROWS)], g.at[1], ld_sem.at[3]),
        pltpu.make_async_copy(b_hbm, w.at[pl.ds(0, R)], ld_sem.at[4]),
        pltpu.make_async_copy(w_hbm, w.at[pl.ds(R, D_LOCAL)], ld_sem.at[5]),
    ]
    for cp in loads:
        cp.start()

    barrier = pltpu.get_barrier_semaphore()
    peers = [(wi, xh * 4 + ring(z, k)) for k in (1, 2, 3)] + [x_cross, partner]
    for dx in (0, 1):
        for k in range(4):
            if dx or k:
                peers.append(wide_dev(xl if dx == 0 else 1 - xl, ring(y, k), c))
    for dev in peers:
        pl.semaphore_signal(barrier, inc=1, device_id=dev, device_id_type=MESH)
    pl.semaphore_wait(barrier, len(peers))

    g_sends = []

    def g_send(src, dst, dev):
        slot = dst[0] * 2 + dst[1]
        sem = len(g_sends)
        send(src, g.at[slot], g_ss.at[sem], g_rs.at[slot], dev)
        g_sends.append(sem)

    def g_wait(step, kind):
        slot = step * 2 + kind
        arrived(g.at[slot], g_rs.at[slot], g_ss.at[0])

    def unit(step, kind):
        return g.at[step * 2 + kind]

    own0, own1 = g_hbm.at[pl.ds(0, ROWS)], g_hbm.at[pl.ds(ROWS, ROWS)]
    g_send(own0, (2, 0), x_cross)
    g_send(own1, (1, 1), z_next)
    g_send(own0, (1, 0), z_prev)

    def spread_own(buf, ss, rs):
        me = buf.at[wi]
        send(me, me, ss.at[0], rs.at[wi], x_pair)
        for k in (1, 3, 2):
            send(me, me, ss.at[k], rs.at[wi], wide_dev(xl, ring(y, k), c))
        send(me, me, ss.at[4], rs.at[wi], partner)

    def spread_pair(buf, ss, rs):
        other = wide_id(1 - xl, y, c)
        blk = buf.at[other]
        arrived(blk, rs.at[other], ss.at[0])
        for i, k in enumerate((1, 3, 2)):
            send(blk, blk, ss.at[5 + i], rs.at[other], wide_dev(xl, ring(y, k), c))
        send(blk, blk, ss.at[8], rs.at[other], partner)

    def spread_core(buf, ss, rs):
        i = 9
        for xl_ in (xl, 1 - xl):
            for k in (1, 3, 2):
                other = wide_id(xl_, ring(y, k), c)
                blk = buf.at[other]
                arrived(blk, rs.at[other], ss.at[0])
                send(blk, blk, ss.at[i], rs.at[other], partner)
                i += 1

    def spread_end(buf, ss, rs):
        for xl_ in (0, 1):
            for y_ in range(4):
                other = wide_id(xl_, y_, 1 - c)
                arrived(buf.at[other], rs.at[other], ss.at[0])

    def spread_sent(buf, ss, rs):
        for i in range(15):
            sent(buf.at[wi], ss.at[i], rs.at[wi])

    loads[0].wait()
    spread_own(xs_all, in_ss, in_rs)

    loads[1].wait()
    low = dot_nn(xs_all[wi], a[...])
    for rh in (0, 1):
        for ch in (0, 1):
            lp[rh * 2 + ch] = low[rh * 56:rh * 56 + 56, ch * 128:ch * 128 + 128]

    def low_stage1():
        for k in (1, 3, 2):
            q = ring(z, k)
            send(lp.at[q], l1.at[3 - k], l1_ss.at[k - 1], l1_rs.at[3 - k], (wi, xh * 4 + q))

    def low_stage2():
        for k in range(3):
            arrived(l1.at[k], l1_rs.at[k], l1_ss.at[k])
        l2s[...] = lp[z] + l1[0] + l1[1] + l1[2]
        send(l2s, l2r, l2_ss, l2_rs, x_cross)

    def low_stage3():
        arrived(l2r, l2_rs, l2_ss)
        lo[z] = l2s[...] + l2r[...]
        for k in (1, 3, 2):
            send(lo.at[z], lo.at[z], l3_ss.at[k - 1], l3_rs.at[z], (wi, xh * 4 + ring(z, k)))

    def low_stage4():
        for k in (1, 2, 3):
            q = ring(z, k)
            arrived(lo.at[q], l3_rs.at[q], l3_ss.at[k - 1])
        top = jnp.concatenate([lo[0], lo[1]], axis=1)
        bottom = jnp.concatenate([lo[2], lo[3]], axis=1)
        la[wi] = jnp.concatenate([top, bottom], axis=0).astype(BF16)
        spread_own(la, la_ss, la_rs)

    low_stage1()
    g_send(own0, (3, 0), z_next)
    g_send(own1, (2, 1), z_prev)

    for cp in loads[2:]:
        cp.wait()

    def owner(step):
        flip, dz = (
            pick(step, [t[i] for t in ORDER[0]]) * (1 - c) + pick(step, [t[i] for t in ORDER[1]]) * c
            for i in (0, 1)
        )
        return (xh + flip) % 2, ring(z, dz)

    def tiles(part):
        return pl.ds(part * PER_PART, PER_PART)

    def send_part(step, part):
        send(part_send.at[step, tiles(part)], part_recv.at[step, tiles(part)],
             c_ss.at[step, part], c_rs.at[step, part], partner)

    def join_cores(step, part):
        xl_n, y_n = owner(step)
        ref = part_recv.at[step, tiles(part)]
        arrived(ref, c_rs.at[step, part], c_ss.at[step, part])

        @pl.when(y_n == y)
        def _():
            for i in range(PER_PART):
                t = part * PER_PART + i
                y_own[xl_n, t] = mine[step % 2, t] + part_recv[step, t].astype(F32)

        @pl.when(y_n != y)
        def _():
            for i in range(PER_PART):
                t = part * PER_PART + i
                part_recv[step, t] = (mine[step % 2, t] + part_recv[step, t].astype(F32)).astype(BF16)
            r = (y - y_n + 4) % 4 - 1
            send(ref, y_recv.at[r, xl_n, tiles(part)], y_ss.at[step, part], y_rs.at[r, xl_n, part],
                 wide_dev(xl, y_n, c))

    def join_y(step, part):
        xl_n, y_n = owner(step)

        @pl.when(y_n == y)
        def _():
            for r in range(3):
                arrived(y_recv.at[r, xl_n, tiles(part)], y_rs.at[r, xl_n, part], x_ss.at[part])

            @pl.when(xl_n == xl)
            def _():
                for i in range(PER_PART):
                    t = part * PER_PART + i
                    y_own[xl_n, t] += (y_recv[0, xl_n, t].astype(F32) + y_recv[1, xl_n, t].astype(F32)
                                       + y_recv[2, xl_n, t].astype(F32))

            @pl.when(xl_n != xl)
            def _():
                for i in range(PER_PART):
                    t = part * PER_PART + i
                    x_send[t] = (y_own[xl_n, t] + y_recv[0, xl_n, t].astype(F32)
                                 + y_recv[1, xl_n, t].astype(F32) + y_recv[2, xl_n, t].astype(F32)).astype(BF16)
                send(x_send.at[tiles(part)], x_recv.at[tiles(part)], x_ss.at[part], x_rs.at[part], x_pair)

    def join_y_all(step):
        for part in range(PARTS):
            join_y(step, part)

    def before(step):
        if step == 1:
            g_wait(1, 0)
            g_wait(1, 1)
            low_stage2()
            g_send(unit(1, 0), (4, 0), x_cross)
            g_send(unit(1, 1), (4, 1), x_cross)
            g_send(own1, (5, 1), x_cross)
        if step == 2:
            g_wait(2, 0)
            low_stage3()
            g_wait(3, 0)
            g_send(unit(3, 0), (5, 0), z_next)
            g_wait(2, 1)
            g_send(unit(2, 1), (3, 1), z_prev)
            spread_pair(xs_all, in_ss, in_rs)
        if step == 3:
            g_wait(4, 0)
            g_send(unit(4, 0), (6, 0), z_prev)
            low_stage4()
            g_wait(3, 1)
        if step == 4:
            g_wait(4, 1)
            g_send(unit(4, 1), (6, 1), z_next)
            g_send(unit(2, 0), (7, 0), z_next)
            spread_pair(la, la_ss, la_rs)
        if step == 5:
            g_wait(5, 0)
            g_wait(5, 1)
            g_send(unit(5, 1), (7, 1), z_prev)
            spread_core(xs_all, in_ss, in_rs)
            spread_core(la, la_ss, la_rs)
        if step == 6:
            g_wait(6, 0)
            g_wait(6, 1)
        if step == 7:
            spread_end(la, la_ss, la_rs)
            for s in range(STEPS):
                for kind in (0, 1):
                    flip, dz = ORDER[kind][s]
                    n = ((xh + flip) % 2) * 4 + ring(z, dz)
                    la_t[pl.ds((s * 2 + kind) * ROWS, ROWS), :] = la[n * 2 + kind]
            g_wait(7, 0)
            g_wait(7, 1)

    def step_body(step, carry):
        for k in range(1, STEPS):
            @pl.when(step == k)
            def _(k=k):
                before(k)

        def tile_body(t, carry):
            rows = g[pl.ds(step * 2, 2)].reshape(2 * ROWS, F_LOCAL)
            cols = w[pl.ds(pl.multiple_of(t * TILE, TILE), TILE), :]
            acc = dot_nt(rows, cols)
            top, bottom = acc[:ROWS], acc[ROWS:]
            mine[step % 2, t] = jnp.where(c == 0, top, bottom)
            part_send[step, t] = jnp.where(c == 0, bottom, top).astype(BF16)

            @pl.when(t == 3)
            def _():
                send_part(step, 0)

            @pl.when(t == 5)
            def _():
                join_cores(step, 0)

            @pl.when(t == 6)
            def _():
                send_part(step, 1)

            @pl.when(t == 8)
            def _():
                join_cores(step, 1)

            return carry

        lax.fori_loop(0, TILES, tile_body, 0)
        send_part(step, 2)
        join_cores(step, 2)

        @pl.when(step == 5)
        def _():
            def early(s, carry):
                join_y_all(s)
                return carry

            lax.fori_loop(0, 5, early, 0)

        @pl.when(step == 6)
        def _():
            join_y_all(5)

        return carry

    lax.fori_loop(0, STEPS, step_body, 0)
    join_y_all(6)
    join_y_all(7)

    arrived(x_recv.at[tiles(0)], x_rs.at[0], x_ss.at[0])
    lg[wi] = (y_own[xl, 0] + x_recv[0].astype(F32)).astype(BF16)
    me = lg.at[wi]
    send(me, me, lg_ss.at[0], lg_rs.at[wi], partner)
    chips = [(dx, k) for dx in (0, 1) for k in (1, 3, 2, 0) if dx or k]
    for i, (dx, k) in enumerate(chips):
        send(me, me, lg_ss.at[1 + i], lg_rs.at[wi], wide_dev(xl if dx == 0 else 1 - xl, ring(y, k), c))

    scale = ADAPTER_SCALE / (16 * ROWS)

    lg_t[...] = la_t[...].T

    def gb_body(t, carry):
        cols = pl.ds(pl.multiple_of(t * TILE, TILE), TILE)
        tokens = g[:, :, cols].reshape(16 * ROWS, TILE)
        gb_ref[:, cols] = scale * dot_nn(lg_t[...], tokens)
        return carry

    lax.fori_loop(0, F_LOCAL // TILE, gb_body, 0)

    for i, (dx, k) in enumerate(chips):
        other = wide_id(xl if dx == 0 else 1 - xl, ring(y, k), c)
        blk = lg.at[other]
        arrived(blk, lg_rs.at[other], lg_ss.at[0])
        send(blk, blk, lg_ss.at[8 + i], lg_rs.at[other], partner)

    for part in range(1, PARTS):
        arrived(x_recv.at[tiles(part)], x_rs.at[part], x_ss.at[part])
    low_rows = lg[wi]

    def ig_body(t, carry):
        cols = pl.ds(pl.multiple_of(t * TILE, TILE), TILE)
        base = y_own[xl, t + 1] + x_recv[t + 1].astype(F32)
        ig_ref[:, cols] = (base + ADAPTER_SCALE * dot_nt(low_rows, a[cols, :])).astype(BF16)
        return carry

    lax.fori_loop(0, D_LOCAL // TILE, ig_body, 0)

    spread_end(xs_all, in_ss, in_rs)
    for xl_ in (0, 1):
        for y_ in range(4):
            other = wide_id(xl_, y_, 1 - c)
            arrived(lg.at[other], lg_rs.at[other], lg_ss.at[0])
    lg_t[...] = lg[...].reshape(16 * ROWS, R).T

    def ga_body(t, carry):
        cols = pl.ds(pl.multiple_of(t * TILE, TILE), TILE)
        tokens = xs_all[:, :, cols].reshape(16 * ROWS, TILE)
        ga_ref[:, cols] = scale * dot_nn(lg_t[...], tokens)
        return carry

    lax.fori_loop(0, D_LOCAL // TILE, ga_body, 0)

    for sem in g_sends:
        sent(g.at[0], g_ss.at[sem], g_rs.at[0])
    for k in range(3):
        sent(lp.at[0], l1_ss.at[k], l1_rs.at[k])
        sent(lo.at[0], l3_ss.at[k], l3_rs.at[k])
    sent(l2s, l2_ss, l2_rs)
    spread_sent(xs_all, in_ss, in_rs)
    spread_sent(la, la_ss, la_rs)
    spread_sent(lg, lg_ss, lg_rs)

    def drain(step, carry):
        xl_n, y_n = owner(step)
        for part in range(PARTS):
            sent(part_send.at[step, tiles(part)], c_ss.at[step, part], c_rs.at[step, part])

            @pl.when(y_n != y)
            def _(part=part):
                sent(part_recv.at[step, tiles(part)], y_ss.at[step, part], y_rs.at[0, 0, part])

        return carry

    lax.fori_loop(0, STEPS, drain, 0)
    for part in range(PARTS):
        sent(x_send.at[tiles(part)], x_ss.at[part], x_rs.at[part])


def shards(inputs, grad_out, w_base, adapter_down_matrix, b_factor):
    dma = pltpu.SemaphoreType.DMA
    scratch = [
        pltpu.VMEM((16, ROWS, F_LOCAL), BF16),
        pltpu.VMEM((R + D_LOCAL, F_LOCAL), BF16),
        pltpu.VMEM((D_LOCAL, R), BF16),
        pltpu.VMEM((16, ROWS, D_LOCAL), BF16),
        pltpu.VMEM((STEPS, TILES, ROWS, TILE), BF16),
        pltpu.VMEM((STEPS, TILES, ROWS, TILE), BF16),
        pltpu.VMEM((2, TILES, ROWS, TILE), F32),
        pltpu.VMEM((3, 2, TILES, ROWS, TILE), BF16),
        pltpu.VMEM((2, TILES, ROWS, TILE), F32),
        pltpu.VMEM((TILES, ROWS, TILE), BF16),
        pltpu.VMEM((TILES, ROWS, TILE), BF16),
        pltpu.VMEM((4, 56, 128), F32),
        pltpu.VMEM((3, 56, 128), F32),
        pltpu.VMEM((56, 128), F32),
        pltpu.VMEM((56, 128), F32),
        pltpu.VMEM((4, 56, 128), F32),
        pltpu.VMEM((16, ROWS, R), BF16),
        pltpu.VMEM((16 * ROWS, R), BF16),
        pltpu.VMEM((16, ROWS, R), BF16),
        pltpu.VMEM((R, 16 * ROWS), BF16),
        dma((6,)), dma((14,)), dma((16,)), dma((STEPS, PARTS)), dma((STEPS, PARTS)),
        dma((STEPS, PARTS)), dma((3, 2, PARTS)), dma((PARTS,)), dma((PARTS,)),
        dma((15,)), dma((16,)), dma((15,)), dma((16,)), dma((15,)), dma((16,)),
        dma((3,)), dma((3,)), dma(()), dma(()), dma((3,)), dma((4,)),
    ]
    any_spec = pl.BlockSpec(memory_space=pl.ANY)
    vmem_spec = pl.BlockSpec(memory_space=pltpu.VMEM)
    input_gradient, grad_a, grad_b = pl.pallas_call(
        kernel,
        out_shape=(
            jax.ShapeDtypeStruct((ROWS, D_LOCAL), BF16),
            jax.ShapeDtypeStruct((R, D_LOCAL), F32),
            jax.ShapeDtypeStruct((R, F_LOCAL), F32),
        ),
        in_specs=[any_spec] * 5,
        out_specs=(vmem_spec,) * 3,
        scratch_shapes=scratch,
        compiler_params=pltpu.CompilerParams(
            collective_id=0, has_side_effects=True, vmem_limit_bytes=67043328
        ),
        name="backward",
    )(inputs, grad_out, w_base, adapter_down_matrix, b_factor)
    return input_gradient, grad_a.T, grad_b


def solution(mesh):
    return jax.shard_map(
        shards,
        mesh=mesh,
        in_specs=(
            P("wide", "narrow"),
            P("narrow", "wide"),
            P("narrow", "wide"),
            P("narrow", None),
            P(None, "wide"),
        ),
        out_specs=(P("wide", "narrow"), P("narrow", None), P(None, "wide")),
        check_vma=False,
    )
```

```python
import jax
import jax.numpy as jnp
from jax import lax
from jax.experimental import pallas as pl
from jax.experimental.pallas import tpu as pltpu
from jax.sharding import PartitionSpec as P

ADAPTER_SCALE = 2.0
ROWS = 112
F_LOCAL = 3328
D_LOCAL = 2048
R = 256
TILE = 256
TILES = (R + D_LOCAL) // TILE
PARTS = 3
PER_PART = TILES // PARTS
HALF = TILE // 2
PASSED = (0, 0, 0, 1, 2, 2, 5, 6, 7)
CUTS = ((0, 64), (64, 48))
STEPS = 8
MESH = pl.DeviceIdType.MESH
BF16 = jnp.bfloat16
F32 = jnp.float32

ORDER = (
    ((0, 0), (0, 1), (1, 0), (0, 3), (1, 3), (1, 1), (0, 2), (1, 2)),
    ((0, 0), (0, 3), (0, 1), (1, 0), (0, 2), (1, 1), (1, 3), (1, 2)),
)


def dot_nt(a, b):
    return lax.dot_general(a, b, (((1,), (1,)), ((), ())), preferred_element_type=F32)


def dot_nn(a, b):
    return lax.dot_general(a, b, (((1,), (0,)), ((), ())), preferred_element_type=F32)


def pick(index, values):
    if isinstance(index, int):
        return values[index]
    out = index * 0 + values[0]
    for i, value in enumerate(values[1:STEPS], 1):
        out = out + (index == i).astype(jnp.int32) * (value - values[0])
    return out


def kernel(
    x_hbm, g_hbm, w_hbm, a_hbm, b_hbm,
    ig_ref, ga_ref, gb_ref,
    g, w, a, xs_all, part_send, part_recv, mine, relay, y_recv, y_own, x_send, x_recv,
    lp, l1, l2s, l2r, lo, la, la_t, lg, lg_t,
    ld_sem, g_ss, g_rs, c_ss, c_rs, f_rs, y_ss, y_rs, x_ss, x_rs,
    in_ss, in_rs, la_ss, la_rs, lg_ss, lg_rs, l1_ss, l1_rs, l2_ss, l2_rs, l3_ss, l3_rs,
):
    wi = lax.axis_index("wide")
    ni = lax.axis_index("narrow")
    xl, y, c = wi // 8, (wi // 2) % 4, wi % 2
    xh, z = ni // 4, ni % 4

    def wide_id(xl_, y_, c_):
        return (xl_ * 4 + y_) * 2 + c_

    def ring(v, k):
        return (v + k) % 4

    def wide_dev(xl_, y_, c_):
        return (wide_id(xl_, y_, c_), ni)

    partner = wide_dev(xl, y, 1 - c)
    x_pair = wide_dev(1 - xl, y, c)
    x_cross = (wi, (1 - xh) * 4 + z)
    z_next = (wi, xh * 4 + ring(z, 1))
    z_prev = (wi, xh * 4 + ring(z, 3))

    def send(src, dst, ss, rs, dev):
        cp = pltpu.make_async_remote_copy(
            src_ref=src, dst_ref=dst, send_sem=ss, recv_sem=rs, device_id=dev, device_id_type=MESH
        )
        cp.start()
        return cp

    def arrived(dst, rs, ss):
        pltpu.make_async_remote_copy(
            src_ref=dst, dst_ref=dst, send_sem=ss, recv_sem=rs, device_id=partner, device_id_type=MESH
        ).wait_recv()

    def sent(src, ss, rs):
        pltpu.make_async_remote_copy(
            src_ref=src, dst_ref=src, send_sem=ss, recv_sem=rs, device_id=partner, device_id_type=MESH
        ).wait_send()

    loads = [
        pltpu.make_async_copy(x_hbm, xs_all.at[wi], ld_sem.at[0]),
        pltpu.make_async_copy(a_hbm, a, ld_sem.at[1]),
        pltpu.make_async_copy(g_hbm.at[pl.ds(0, ROWS)], g.at[0], ld_sem.at[2]),
        pltpu.make_async_copy(g_hbm.at[pl.ds(ROWS, ROWS)], g.at[1], ld_sem.at[3]),
        pltpu.make_async_copy(b_hbm, w.at[pl.ds(0, R)], ld_sem.at[4]),
        pltpu.make_async_copy(w_hbm, w.at[pl.ds(R, D_LOCAL)], ld_sem.at[5]),
    ]
    for cp in loads:
        cp.start()

    barrier = pltpu.get_barrier_semaphore()
    peers = [(wi, xh * 4 + ring(z, k)) for k in (1, 2, 3)] + [x_cross, partner]
    for dx in (0, 1):
        for k in range(4):
            if dx or k:
                peers.append(wide_dev(xl if dx == 0 else 1 - xl, ring(y, k), c))
    for dev in peers:
        pl.semaphore_signal(barrier, inc=1, device_id=dev, device_id_type=MESH)
    pl.semaphore_wait(barrier, len(peers))

    g_sends = []

    def g_slot(unit, cut):
        slot = unit[0] * 2 + unit[1]
        if cut is None:
            return g.at[slot], slot
        return g.at[slot, pl.ds(*CUTS[cut])], slot if cut == 0 else 16 + unit[0] - 6

    def g_send(src, dst, dev, cut=None):
        ref, sem = g_slot(dst, cut)
        if isinstance(src, tuple):
            src = g_slot(src, cut)[0]
        elif cut is not None:
            src = src.at[pl.ds(*CUTS[cut])]
        send(src, ref, g_ss.at[len(g_sends)], g_rs.at[sem], dev)
        g_sends.append(cut)

    def g_wait(step, kind, cut=None):
        ref, sem = g_slot((step, kind), cut)
        arrived(ref, g_rs.at[sem], g_ss.at[0])

    own0, own1 = g_hbm.at[pl.ds(0, ROWS)], g_hbm.at[pl.ds(ROWS, ROWS)]
    g_send(own0, (2, 0), x_cross)
    g_send(own1, (1, 1), z_next)
    g_send(own0, (1, 0), z_prev)

    def spread_own(buf, ss, rs):
        me = buf.at[wi]
        send(me, me, ss.at[0], rs.at[wi], x_pair)
        for k in (1, 3, 2):
            send(me, me, ss.at[k], rs.at[wi], wide_dev(xl, ring(y, k), c))
        send(me, me, ss.at[4], rs.at[wi], partner)

    def spread_pair(buf, ss, rs):
        other = wide_id(1 - xl, y, c)
        blk = buf.at[other]
        arrived(blk, rs.at[other], ss.at[0])
        for i, k in enumerate((1, 3, 2)):
            send(blk, blk, ss.at[5 + i], rs.at[other], wide_dev(xl, ring(y, k), c))
        send(blk, blk, ss.at[8], rs.at[other], partner)

    def spread_core(buf, ss, rs):
        i = 9
        for xl_ in (xl, 1 - xl):
            for k in (1, 3, 2):
                other = wide_id(xl_, ring(y, k), c)
                blk = buf.at[other]
                arrived(blk, rs.at[other], ss.at[0])
                send(blk, blk, ss.at[i], rs.at[other], partner)
                i += 1

    def spread_end(buf, ss, rs):
        for xl_ in (0, 1):
            for y_ in range(4):
                other = wide_id(xl_, y_, 1 - c)
                arrived(buf.at[other], rs.at[other], ss.at[0])

    def spread_sent(buf, ss, rs):
        for i in range(15):
            sent(buf.at[wi], ss.at[i], rs.at[wi])

    loads[0].wait()
    spread_own(xs_all, in_ss, in_rs)

    loads[1].wait()
    low = dot_nn(xs_all[wi], a[...])
    for rh in (0, 1):
        for ch in (0, 1):
            lp[rh * 2 + ch] = low[rh * 56:rh * 56 + 56, ch * 128:ch * 128 + 128]

    def low_stage1():
        for k in (1, 3, 2):
            q = ring(z, k)
            send(lp.at[q], l1.at[3 - k], l1_ss.at[k - 1], l1_rs.at[3 - k], (wi, xh * 4 + q))

    def low_stage2():
        for k in range(3):
            arrived(l1.at[k], l1_rs.at[k], l1_ss.at[k])
        l2s[...] = lp[z] + l1[0] + l1[1] + l1[2]
        send(l2s, l2r, l2_ss, l2_rs, x_cross)

    def low_stage3():
        arrived(l2r, l2_rs, l2_ss)
        lo[z] = l2s[...] + l2r[...]
        for k in (1, 3, 2):
            send(lo.at[z], lo.at[z], l3_ss.at[k - 1], l3_rs.at[z], (wi, xh * 4 + ring(z, k)))

    def low_stage4():
        for k in (1, 2, 3):
            q = ring(z, k)
            arrived(lo.at[q], l3_rs.at[q], l3_ss.at[k - 1])
        top = jnp.concatenate([lo[0], lo[1]], axis=1)
        bottom = jnp.concatenate([lo[2], lo[3]], axis=1)
        la[wi] = jnp.concatenate([top, bottom], axis=0).astype(BF16)
        spread_own(la, la_ss, la_rs)

    low_stage1()
    g_send(own1, (3, 1), x_cross)
    g_send(own0, (3, 0), z_next)
    g_send(own1, (2, 1), z_prev)

    for cp in loads[2:]:
        cp.wait()

    def owner(step):
        flip, dz = (
            pick(step, [t[i] for t in ORDER[0]]) * (1 - c) + pick(step, [t[i] for t in ORDER[1]]) * c
            for i in (0, 1)
        )
        return (xh + flip) % 2, ring(z, dz)

    def send_part(step, part):
        send(part_send.at[step, part], part_recv.at[step, part],
             c_ss.at[step, part], c_rs.at[step, part], partner)

    def join_cores(step, part):
        xl_n, y_n = owner(step)
        d = (y - y_n + 4) % 4
        arrived(part_recv.at[step, part], c_rs.at[step, part], c_ss.at[step, part])

        def total(h, i):
            return mine[step % 4, part, h, i] + part_recv[step, part, h, i].astype(F32)

        @pl.when(d == 0)
        def _():
            for h in (0, 1):
                for i in range(PER_PART):
                    y_own[xl_n, part, h, i] = total(h, i)

        @pl.when(d == 2)
        def _():
            for h in (0, 1):
                for i in range(PER_PART):
                    part_recv[step, part, h, i] = total(h, i).astype(BF16)
            for h, k in ((0, 3), (1, 1)):
                send(part_recv.at[step, part, h], relay.at[h, xl_n, part], y_ss.at[step, part, h],
                     f_rs.at[h, xl_n, part], wide_dev(xl, ring(y, k), c))

        @pl.when(d % 2 == 1)
        def _():
            late = d // 2
            for i in range(PER_PART):
                mine[step % 4, part, late, i] = total(late, i)
                part_recv[step, part, 1 - late, i] = total(1 - late, i).astype(BF16)
            send(part_recv.at[step, part, 1 - late], y_recv.at[late, xl_n, part, 1 - late],
                 y_ss.at[step, part, 1 - late], y_rs.at[late, xl_n, part, 1 - late], wide_dev(xl, y_n, c))

    def pass_on(step, part):
        xl_n, y_n = owner(step)
        d = (y - y_n + 4) % 4

        @pl.when(d % 2 == 1)
        def _():
            late = d // 2
            arrived(relay.at[late, xl_n, part], f_rs.at[late, xl_n, part], x_ss.at[part])
            for i in range(PER_PART):
                part_recv[step, part, late, i] = (
                    mine[step % 4, part, late, i] + relay[late, xl_n, part, i].astype(F32)
                ).astype(BF16)
            send(part_recv.at[step, part, late], y_recv.at[late, xl_n, part, late],
                 y_ss.at[step, part, late], y_rs.at[late, xl_n, part, late], wide_dev(xl, y_n, c))

    def join_y(step, part):
        xl_n, y_n = owner(step)

        @pl.when(y_n == y)
        def _():
            for r in (0, 1):
                for h in (0, 1):
                    arrived(y_recv.at[r, xl_n, part, h], y_rs.at[r, xl_n, part, h], x_ss.at[part])

            def total(h, i):
                return (y_own[xl_n, part, h, i] + y_recv[0, xl_n, part, h, i].astype(F32)
                        + y_recv[1, xl_n, part, h, i].astype(F32))

            @pl.when(xl_n == xl)
            def _():
                for h in (0, 1):
                    for i in range(PER_PART):
                        y_own[xl_n, part, h, i] = total(h, i)

            @pl.when(xl_n != xl)
            def _():
                for h in (0, 1):
                    for i in range(PER_PART):
                        x_send[part, h, i] = total(h, i).astype(BF16)
                send(x_send.at[part], x_recv.at[part], x_ss.at[part], x_rs.at[part], x_pair)

    def over_parts(do, step):
        def body(part, carry):
            do(step, part)
            return carry

        return lax.fori_loop(0, PARTS, body, 0)

    def pass_on_all(step):
        return over_parts(pass_on, step)

    def join_y_all(step):
        return over_parts(join_y, step)

    def own_total(part, h, i):
        return y_own[xl, part, h, i] + x_recv[part, h, i].astype(F32)

    def before(step):
        if step == 1:
            g_wait(1, 0)
            low_stage2()
            g_send((1, 0), (5, 0), x_cross)
            g_wait(1, 1)
            g_send(g.at[3], (6, 1), x_cross, 0)
            g_send(g.at[3], (6, 1), x_cross, 1)
        if step == 2:
            g_wait(2, 0)
            g_send((2, 0), (4, 0), z_next)
            g_wait(2, 1)
            g_send((2, 1), (4, 1), z_prev)
            g_wait(3, 0)
            g_send((3, 0), (6, 0), z_next)
            spread_pair(xs_all, in_ss, in_rs)
        if step == 3:
            g_wait(3, 1)
            g_send((3, 1), (5, 1), z_prev)
            low_stage3()
        if step == 4:
            g_wait(4, 0)
            g_wait(4, 1)
        if step == 5:
            g_wait(5, 0)
            g_send((5, 0), (7, 0), z_prev)
            spread_core(xs_all, in_ss, in_rs)
            g_wait(6, 1, 0)
            g_send((6, 1), (7, 1), z_next, 0)
            g_wait(5, 1)
            low_stage4()
        if step == 6:
            g_wait(6, 0)
            g_wait(6, 1, 1)
            g_send((6, 1), (7, 1), z_next, 1)
            spread_pair(la, la_ss, la_rs)
        if step == 7:
            spread_core(la, la_ss, la_rs)
            g_wait(7, 0)
            g_wait(7, 1, 0)
            g_wait(7, 1, 1)

    def step_body(step, carry):
        for k in range(1, STEPS):
            @pl.when(step == k)
            def _(k=k):
                before(k)

        def tile_body(t, carry):
            rows = g[pl.ds(step * 2, 2)].reshape(2 * ROWS, F_LOCAL)
            cols = w[pl.ds(pl.multiple_of(t * TILE, TILE), TILE), :]
            acc = dot_nt(rows, cols)
            top, bottom = acc[:ROWS], acc[ROWS:]
            keep, give = jnp.where(c == 0, top, bottom), jnp.where(c == 0, bottom, top).astype(BF16)
            part, i = t // PER_PART, t % PER_PART
            for h in (0, 1):
                mine[step % 4, part, h, i] = keep[:, h * HALF:h * HALF + HALF]
                part_send[step, part, h, i] = give[:, h * HALF:h * HALF + HALF]

            @pl.when(t == 4)
            def _():
                lax.fori_loop(pick(step, PASSED), pick(step, PASSED[1:]), lambda s, carry: pass_on_all(s), 0)

            @pl.when(((t == 8) & (step == 6)) | ((t == 4) & (step == 7)))
            def _():
                join_y_all(step - 2)

            @pl.when(t == 3)
            def _():
                send_part(step, 0)

            @pl.when((t == 5) | (t == 8))
            def _():
                join_cores(step, t // 4 - 1)

            @pl.when(t == 6)
            def _():
                send_part(step, 1)

            return carry

        lax.fori_loop(0, TILES, tile_body, 0)
        send_part(step, 2)
        join_cores(step, 2)

        @pl.when(step == 5)
        def _():
            def early(s, carry):
                join_y_all(s)
                return carry

            lax.fori_loop(0, 4, early, 0)

        return carry

    lax.fori_loop(0, STEPS, step_body, 0)
    pass_on_all(7)
    join_y_all(6)
    join_y_all(7)

    arrived(x_recv.at[0], x_rs.at[0], x_ss.at[0])
    lg[wi] = jnp.concatenate([own_total(0, 0, 0), own_total(0, 1, 0)], axis=1).astype(BF16)
    me = lg.at[wi]
    send(me, me, lg_ss.at[0], lg_rs.at[wi], partner)
    chips = [(dx, k) for dx in (0, 1) for k in (1, 3, 2, 0) if dx or k]
    for i, (dx, k) in enumerate(chips):
        send(me, me, lg_ss.at[1 + i], lg_rs.at[wi], wide_dev(xl if dx == 0 else 1 - xl, ring(y, k), c))

    scale = ADAPTER_SCALE / (16 * ROWS)

    spread_end(la, la_ss, la_rs)
    for s in range(STEPS):
        for kind in (0, 1):
            flip, dz = ORDER[kind][s]
            n = ((xh + flip) % 2) * 4 + ring(z, dz)
            la_t[pl.ds((s * 2 + kind) * ROWS, ROWS), :] = la[n * 2 + kind]
    lg_t[...] = la_t[...].T

    def gb_body(t, carry):
        cols = pl.ds(pl.multiple_of(t * TILE, TILE), TILE)
        tokens = g[:, :, cols].reshape(16 * ROWS, TILE)
        gb_ref[:, cols] = scale * dot_nn(lg_t[...], tokens)
        return carry

    lax.fori_loop(0, F_LOCAL // TILE, gb_body, 0)

    for i, (dx, k) in enumerate(chips):
        other = wide_id(xl if dx == 0 else 1 - xl, ring(y, k), c)
        blk = lg.at[other]
        arrived(blk, lg_rs.at[other], lg_ss.at[0])
        send(blk, blk, lg_ss.at[8 + i], lg_rs.at[other], partner)

    for part in range(1, PARTS):
        arrived(x_recv.at[part], x_rs.at[part], x_ss.at[part])
    low_rows = lg[wi]

    def ig_body(t, carry):
        cols = pl.ds(pl.multiple_of(t * TILE, TILE), TILE)
        part, i = (t + 1) // PER_PART, (t + 1) % PER_PART
        base = jnp.concatenate([own_total(part, 0, i), own_total(part, 1, i)], axis=1)
        ig_ref[:, cols] = (base + ADAPTER_SCALE * dot_nt(low_rows, a[cols, :])).astype(BF16)
        return carry

    lax.fori_loop(0, D_LOCAL // TILE, ig_body, 0)

    spread_end(xs_all, in_ss, in_rs)
    for xl_ in (0, 1):
        for y_ in range(4):
            other = wide_id(xl_, y_, 1 - c)
            arrived(lg.at[other], lg_rs.at[other], lg_ss.at[0])
    lg_t[...] = lg[...].reshape(16 * ROWS, R).T

    def ga_body(t, carry):
        cols = pl.ds(pl.multiple_of(t * TILE, TILE), TILE)
        tokens = xs_all[:, :, cols].reshape(16 * ROWS, TILE)
        ga_ref[:, cols] = scale * dot_nn(lg_t[...], tokens)
        return carry

    lax.fori_loop(0, D_LOCAL // TILE, ga_body, 0)

    for sem, cut in enumerate(g_sends):
        sent(g_slot((0, 0), None)[0] if cut is None else g.at[0, pl.ds(*CUTS[cut])], g_ss.at[sem], g_rs.at[0])
    for k in range(3):
        sent(lp.at[0], l1_ss.at[k], l1_rs.at[k])
        sent(lo.at[0], l3_ss.at[k], l3_rs.at[k])
    sent(l2s, l2_ss, l2_rs)
    spread_sent(xs_all, in_ss, in_rs)
    spread_sent(la, la_ss, la_rs)
    spread_sent(lg, lg_ss, lg_rs)

    def drain(step, carry):
        xl_n, y_n = owner(step)
        for part in range(PARTS):
            sent(part_send.at[step, part], c_ss.at[step, part], c_rs.at[step, part])

            @pl.when(y_n != y)
            def _(part=part):
                for h in (0, 1):
                    sent(part_recv.at[step, part, h], y_ss.at[step, part, h], y_rs.at[0, 0, part, h])

        return carry

    lax.fori_loop(0, STEPS, drain, 0)
    for part in range(PARTS):
        sent(x_send.at[part], x_ss.at[part], x_rs.at[part])


def shards(inputs, grad_out, w_base, adapter_down_matrix, b_factor):
    dma = pltpu.SemaphoreType.DMA
    pieces = (PARTS, 2, PER_PART, ROWS, HALF)
    scratch = [
        pltpu.VMEM((16, ROWS, F_LOCAL), BF16),
        pltpu.VMEM((R + D_LOCAL, F_LOCAL), BF16),
        pltpu.VMEM((D_LOCAL, R), BF16),
        pltpu.VMEM((16, ROWS, D_LOCAL), BF16),
        pltpu.VMEM((STEPS,) + pieces, BF16),
        pltpu.VMEM((STEPS,) + pieces, BF16),
        pltpu.VMEM((4,) + pieces, F32),
        pltpu.VMEM((2, 2, PARTS, PER_PART, ROWS, HALF), BF16),
        pltpu.VMEM((2, 2) + pieces, BF16),
        pltpu.VMEM((2,) + pieces, F32),
        pltpu.VMEM(pieces, BF16),
        pltpu.VMEM(pieces, BF16),
        pltpu.VMEM((4, 56, 128), F32),
        pltpu.VMEM((3, 56, 128), F32),
        pltpu.VMEM((56, 128), F32),
        pltpu.VMEM((56, 128), F32),
        pltpu.VMEM((4, 56, 128), F32),
        pltpu.VMEM((16, ROWS, R), BF16),
        pltpu.VMEM((16 * ROWS, R), BF16),
        pltpu.VMEM((16, ROWS, R), BF16),
        pltpu.VMEM((R, 16 * ROWS), BF16),
        dma((6,)), dma((16,)), dma((18,)), dma((STEPS, PARTS)), dma((STEPS, PARTS)),
        dma((2, 2, PARTS)), dma((STEPS, PARTS, 2)), dma((2, 2, PARTS, 2)), dma((PARTS,)), dma((PARTS,)),
        dma((15,)), dma((16,)), dma((15,)), dma((16,)), dma((15,)), dma((16,)),
        dma((3,)), dma((3,)), dma(()), dma(()), dma((3,)), dma((4,)),
    ]
    any_spec = pl.BlockSpec(memory_space=pl.ANY)
    vmem_spec = pl.BlockSpec(memory_space=pltpu.VMEM)
    input_gradient, grad_a, grad_b = pl.pallas_call(
        kernel,
        out_shape=(
            jax.ShapeDtypeStruct((ROWS, D_LOCAL), BF16),
            jax.ShapeDtypeStruct((R, D_LOCAL), F32),
            jax.ShapeDtypeStruct((R, F_LOCAL), F32),
        ),
        in_specs=[any_spec] * 5,
        out_specs=(vmem_spec,) * 3,
        scratch_shapes=scratch,
        compiler_params=pltpu.CompilerParams(
            collective_id=0, has_side_effects=True, vmem_limit_bytes=67043328
        ),
        name="backward",
    )(inputs, grad_out, w_base, adapter_down_matrix, b_factor)
    return input_gradient, grad_a.T, grad_b


def solution(mesh):
    return jax.shard_map(
        shards,
        mesh=mesh,
        in_specs=(
            P("wide", "narrow"),
            P("narrow", "wide"),
            P("narrow", "wide"),
            P("narrow", None),
            P(None, "wide"),
        ),
        out_specs=(P("wide", "narrow"), P("narrow", None), P(None, "wide")),
        check_vma=False,
    )
```

```python
import jax
import jax.numpy as jnp
from jax import lax
from jax.experimental import pallas as pl
from jax.experimental.pallas import tpu as pltpu
from jax.sharding import PartitionSpec as P

ADAPTER_SCALE = 2.0
ROWS = 112
F_LOCAL = 3328
D_LOCAL = 2048
R = 256
TILE = 256
TILES = (R + D_LOCAL) // TILE
PARTS = 3
PER_PART = TILES // PARTS
HALF = TILE // 2
PASSED = (0, 0, 0, 1, 2, 2, 5, 6, 7)
JOINED = (0, 0, 0, 0, 0, 0, 2, 4, 6)
CHIPS = ((0, 1), (0, 3), (0, 2), (1, 0), (1, 1), (1, 3), (1, 2))
CUTS = ((0, 64), (64, 48))
STEPS = 8
MESH = pl.DeviceIdType.MESH
BF16 = jnp.bfloat16
F32 = jnp.float32

ORDER = (
    ((0, 0), (0, 1), (1, 0), (0, 3), (1, 3), (0, 2), (1, 1), (1, 2)),
    ((0, 0), (0, 3), (0, 1), (1, 0), (0, 2), (1, 1), (1, 3), (1, 2)),
)


def dot_nt(a, b):
    return lax.dot_general(a, b, (((1,), (1,)), ((), ())), preferred_element_type=F32)


def dot_nn(a, b):
    return lax.dot_general(a, b, (((1,), (0,)), ((), ())), preferred_element_type=F32)


def pick(index, values):
    if isinstance(index, int):
        return values[index]
    out = index * 0 + values[0]
    for i, value in enumerate(values[1:STEPS], 1):
        out = out + (index == i).astype(jnp.int32) * (value - values[0])
    return out


def kernel(
    x_hbm, g_hbm, w_hbm, a_hbm, b_hbm,
    ig_ref, ga_ref, gb_ref,
    g, w, a, xs_all, part_send, part_recv, mine, relay, y_recv, y_own, x_send, x_recv,
    lp, l1, l2s, l2r, lo, la, la_t, lg, lg_t,
    ld_sem, g_ss, g_rs, c_ss, c_rs, f_rs, y_ss, y_rs, x_ss, x_rs,
    in_ss, in_rs, la_ss, la_rs, lg_ss, lg_rs, l1_ss, l1_rs, l2_ss, l2_rs, l3_ss, l3_rs,
):
    wi = lax.axis_index("wide")
    ni = lax.axis_index("narrow")
    xl, y, c = wi // 8, (wi // 2) % 4, wi % 2
    xh, z = ni // 4, ni % 4

    def wide_id(xl_, y_, c_):
        return (xl_ * 4 + y_) * 2 + c_

    def ring(v, k):
        return (v + k) % 4

    def wide_dev(xl_, y_, c_):
        return (wide_id(xl_, y_, c_), ni)

    partner = wide_dev(xl, y, 1 - c)
    x_pair = wide_dev(1 - xl, y, c)
    x_cross = (wi, (1 - xh) * 4 + z)
    z_next = (wi, xh * 4 + ring(z, 1))
    z_prev = (wi, xh * 4 + ring(z, 3))

    def send(src, dst, ss, rs, dev):
        cp = pltpu.make_async_remote_copy(
            src_ref=src, dst_ref=dst, send_sem=ss, recv_sem=rs, device_id=dev, device_id_type=MESH
        )
        cp.start()
        return cp

    def arrived(dst, rs, ss):
        pltpu.make_async_remote_copy(
            src_ref=dst, dst_ref=dst, send_sem=ss, recv_sem=rs, device_id=partner, device_id_type=MESH
        ).wait_recv()

    def sent(src, ss, rs):
        pltpu.make_async_remote_copy(
            src_ref=src, dst_ref=src, send_sem=ss, recv_sem=rs, device_id=partner, device_id_type=MESH
        ).wait_send()

    loads = [
        pltpu.make_async_copy(x_hbm, xs_all.at[wi], ld_sem.at[0]),
        pltpu.make_async_copy(a_hbm, a, ld_sem.at[1]),
        pltpu.make_async_copy(g_hbm.at[pl.ds(0, ROWS)], g.at[0], ld_sem.at[2]),
        pltpu.make_async_copy(g_hbm.at[pl.ds(ROWS, ROWS)], g.at[1], ld_sem.at[3]),
        pltpu.make_async_copy(b_hbm, w.at[pl.ds(0, R)], ld_sem.at[4]),
        pltpu.make_async_copy(w_hbm, w.at[pl.ds(R, D_LOCAL)], ld_sem.at[5]),
    ]
    for cp in loads:
        cp.start()

    barrier = pltpu.get_barrier_semaphore()
    peers = [(wi, xh * 4 + ring(z, k)) for k in (1, 2, 3)] + [x_cross, partner]
    for dx in (0, 1):
        for k in range(4):
            if dx or k:
                peers.append(wide_dev(xl if dx == 0 else 1 - xl, ring(y, k), c))
    for dev in peers:
        pl.semaphore_signal(barrier, inc=1, device_id=dev, device_id_type=MESH)
    pl.semaphore_wait(barrier, len(peers))

    g_sends = []

    def g_slot(unit, cut):
        slot = unit[0] * 2 + unit[1]
        if cut is None:
            return g.at[slot], slot
        return g.at[slot, pl.ds(*CUTS[cut])], slot if cut == 0 else 16 + unit[0] - 6

    def g_send(src, dst, dev, cut=None):
        ref, sem = g_slot(dst, cut)
        if isinstance(src, tuple):
            src = g_slot(src, cut)[0]
        elif cut is not None:
            src = src.at[pl.ds(*CUTS[cut])]
        send(src, ref, g_ss.at[len(g_sends)], g_rs.at[sem], dev)
        g_sends.append(cut)

    def g_wait(step, kind, cut=None):
        ref, sem = g_slot((step, kind), cut)
        arrived(ref, g_rs.at[sem], g_ss.at[0])

    own0, own1 = g_hbm.at[pl.ds(0, ROWS)], g_hbm.at[pl.ds(ROWS, ROWS)]
    g_send(own0, (2, 0), x_cross)
    g_send(own1, (1, 1), z_next)
    g_send(own0, (1, 0), z_prev)

    def spread_own(buf, ss, rs):
        me = buf.at[wi]
        send(me, me, ss.at[0], rs.at[wi], x_pair)
        for k in (1, 3, 2):
            send(me, me, ss.at[k], rs.at[wi], wide_dev(xl, ring(y, k), c))
        send(me, me, ss.at[4], rs.at[wi], partner)

    def spread_pair(buf, ss, rs, near=True, far=True):
        other = wide_id(1 - xl, y, c)
        blk = buf.at[other]
        if near:
            arrived(blk, rs.at[other], ss.at[0])
            send(blk, blk, ss.at[8], rs.at[other], partner)
        for i, k in enumerate((1, 3, 2)):
            if near and k != 2 or far and k == 2:
                send(blk, blk, ss.at[5 + i], rs.at[other], wide_dev(xl, ring(y, k), c))

    def spread_core(buf, ss, rs, blocks=range(6)):
        for i in blocks:
            other = wide_id(xl if i < 3 else 1 - xl, ring(y, (1, 3, 2)[i % 3]), c)
            blk = buf.at[other]
            arrived(blk, rs.at[other], ss.at[0])
            send(blk, blk, ss.at[9 + i], rs.at[other], partner)

    def spread_end(buf, ss, rs):
        for xl_ in (0, 1):
            for y_ in range(4):
                other = wide_id(xl_, y_, 1 - c)
                arrived(buf.at[other], rs.at[other], ss.at[0])

    def spread_sent(buf, ss, rs):
        for i in range(15):
            sent(buf.at[wi], ss.at[i], rs.at[wi])

    loads[0].wait()
    spread_own(xs_all, in_ss, in_rs)

    loads[1].wait()
    low = dot_nn(xs_all[wi], a[...])
    for rh in (0, 1):
        for ch in (0, 1):
            lp[rh * 2 + ch] = low[rh * 56:rh * 56 + 56, ch * 128:ch * 128 + 128]

    def low_stage1():
        for k in (1, 3, 2):
            q = ring(z, k)
            send(lp.at[q], l1.at[3 - k], l1_ss.at[k - 1], l1_rs.at[3 - k], (wi, xh * 4 + q))

    def low_stage2():
        for k in range(3):
            arrived(l1.at[k], l1_rs.at[k], l1_ss.at[k])
        l2s[...] = lp[z] + l1[0] + l1[1] + l1[2]
        send(l2s, l2r, l2_ss, l2_rs, x_cross)

    def low_stage3():
        arrived(l2r, l2_rs, l2_ss)
        lo[z] = l2s[...] + l2r[...]
        for k in (1, 3, 2):
            send(lo.at[z], lo.at[z], l3_ss.at[k - 1], l3_rs.at[z], (wi, xh * 4 + ring(z, k)))

    def low_stage4():
        for k in (1, 2, 3):
            q = ring(z, k)
            arrived(lo.at[q], l3_rs.at[q], l3_ss.at[k - 1])
        top = jnp.concatenate([lo[0], lo[1]], axis=1)
        bottom = jnp.concatenate([lo[2], lo[3]], axis=1)
        la[wi] = jnp.concatenate([top, bottom], axis=0).astype(BF16)
        spread_own(la, la_ss, la_rs)

    low_stage1()
    g_send(own0, (3, 0), z_next)
    g_send(own1, (2, 1), z_prev)

    for cp in loads[2:]:
        cp.wait()

    def owner(step):
        flip, dz = (
            pick(step, [t[i] for t in ORDER[0]]) * (1 - c) + pick(step, [t[i] for t in ORDER[1]]) * c
            for i in (0, 1)
        )
        return (xh + flip) % 2, ring(z, dz)

    def send_part(step, part):
        send(part_send.at[step, part], part_recv.at[step, part],
             c_ss.at[step, part], c_rs.at[step, part], partner)

    def join_cores(step, part):
        xl_n, y_n = owner(step)
        d = (y - y_n + 4) % 4
        arrived(part_recv.at[step, part], c_rs.at[step, part], c_ss.at[step, part])

        def total(h, i):
            return mine[step % 4, part, h, i] + part_recv[step, part, h, i].astype(F32)

        @pl.when(d == 0)
        def _():
            for h in (0, 1):
                for i in range(PER_PART):
                    y_own[xl_n, part, h, i] = total(h, i)

        @pl.when(d == 2)
        def _():
            for h in (0, 1):
                for i in range(PER_PART):
                    part_recv[step, part, h, i] = total(h, i).astype(BF16)
            for h, k in ((0, 3), (1, 1)):
                send(part_recv.at[step, part, h], relay.at[h, xl_n, part], y_ss.at[step, part, h],
                     f_rs.at[h, xl_n, part], wide_dev(xl, ring(y, k), c))

        @pl.when(d % 2 == 1)
        def _():
            late = d // 2
            for i in range(PER_PART):
                mine[step % 4, part, late, i] = total(late, i)
                part_recv[step, part, 1 - late, i] = total(1 - late, i).astype(BF16)
            send(part_recv.at[step, part, 1 - late], y_recv.at[late, xl_n, part, 1 - late],
                 y_ss.at[step, part, 1 - late], y_rs.at[late, xl_n, part, 1 - late], wide_dev(xl, y_n, c))

    def pass_on(step, part):
        xl_n, y_n = owner(step)
        d = (y - y_n + 4) % 4

        @pl.when(d % 2 == 1)
        def _():
            late = d // 2
            arrived(relay.at[late, xl_n, part], f_rs.at[late, xl_n, part], x_ss.at[part])
            for i in range(PER_PART):
                part_recv[step, part, late, i] = (
                    mine[step % 4, part, late, i] + relay[late, xl_n, part, i].astype(F32)
                ).astype(BF16)
            send(part_recv.at[step, part, late], y_recv.at[late, xl_n, part, late],
                 y_ss.at[step, part, late], y_rs.at[late, xl_n, part, late], wide_dev(xl, y_n, c))

    def join_y(step, part):
        xl_n, y_n = owner(step)

        @pl.when(y_n == y)
        def _():
            for r in (0, 1):
                for h in (0, 1):
                    arrived(y_recv.at[r, xl_n, part, h], y_rs.at[r, xl_n, part, h], x_ss.at[part])

            def total(h, i):
                return (y_own[xl_n, part, h, i] + y_recv[0, xl_n, part, h, i].astype(F32)
                        + y_recv[1, xl_n, part, h, i].astype(F32))

            @pl.when(xl_n == xl)
            def _():
                for h in (0, 1):
                    for i in range(PER_PART):
                        y_own[xl_n, part, h, i] = total(h, i)

            @pl.when(xl_n != xl)
            def _():
                for h in (0, 1):
                    for i in range(PER_PART):
                        x_send[part, h, i] = total(h, i).astype(BF16)
                send(x_send.at[part], x_recv.at[part], x_ss.at[part], x_rs.at[part], x_pair)

    def over_parts(do, step):
        def body(part, carry):
            do(step, part)
            return carry

        return lax.fori_loop(0, PARTS, body, 0)

    def pass_on_all(step):
        return over_parts(pass_on, step)

    def join_y_all(step):
        return over_parts(join_y, step)

    def own_total(part, h, i):
        return y_own[xl, part, h, i] + x_recv[part, h, i].astype(F32)

    def announce_all(step):
        xl_n, y_n = owner(step)

        @pl.when((xl_n == xl) & (y_n == y))
        def _():
            arrived(x_recv.at[0], x_rs.at[0], x_ss.at[0])
            lg[wi] = jnp.concatenate([own_total(0, 0, 0), own_total(0, 1, 0)], axis=1).astype(BF16)
            me = lg.at[wi]
            send(me, me, lg_ss.at[0], lg_rs.at[wi], partner)
            for i, (dx, k) in enumerate(CHIPS):
                send(me, me, lg_ss.at[1 + i], lg_rs.at[wi], wide_dev((xl + dx) % 2, ring(y, k), c))

        return 0

    def before(step):
        if step == 1:
            g_wait(1, 0)
            low_stage2()
            g_send(g_hbm.at[pl.ds(ROWS, ROWS)], (3, 1), x_cross)
            g_send((1, 0), (6, 0), x_cross)
            g_wait(1, 1)
            g_send(g.at[3], (6, 1), x_cross, 0)
            g_send(g.at[3], (6, 1), x_cross, 1)
        if step == 2:
            g_wait(2, 0)
            g_send((2, 0), (4, 0), z_next)
            low_stage3()
            g_wait(2, 1)
            g_send((2, 1), (4, 1), z_prev)
            g_wait(3, 0)
            g_send((3, 0), (5, 0), z_next)
            spread_pair(xs_all, in_ss, in_rs, far=False)
        if step == 3:
            g_wait(3, 1)
            g_send((3, 1), (5, 1), z_prev)
            spread_pair(xs_all, in_ss, in_rs, near=False)
        if step == 4:
            g_wait(4, 1)
            g_wait(4, 0)
            low_stage4()
        if step == 5:
            g_wait(6, 0)
            g_send((6, 0), (7, 0), z_prev)
            spread_core(xs_all, in_ss, in_rs, range(3))
            join_y_all(0)
            join_y_all(1)
            g_wait(6, 1, 0)
            g_send((6, 1), (7, 1), z_next, 0)
            g_wait(5, 0)
            g_wait(5, 1)
        if step == 6:
            spread_core(xs_all, in_ss, in_rs, range(3, 6))
            g_wait(6, 1, 1)
            g_send((6, 1), (7, 1), z_next, 1)
            spread_pair(la, la_ss, la_rs)
        if step == 7:
            spread_core(la, la_ss, la_rs)
            g_wait(7, 0)
            g_wait(7, 1, 0)
            g_wait(7, 1, 1)

    def step_body(step, carry):
        for k in range(1, STEPS):
            @pl.when(step == k)
            def _(k=k):
                before(k)

        def tile_body(t, carry):
            rows = g[pl.ds(step * 2, 2)].reshape(2 * ROWS, F_LOCAL)
            cols = w[pl.ds(pl.multiple_of(t * TILE, TILE), TILE), :]
            acc = dot_nt(rows, cols)
            top, bottom = acc[:ROWS], acc[ROWS:]
            keep, give = jnp.where(c == 0, top, bottom), jnp.where(c == 0, bottom, top).astype(BF16)
            part, i = t // PER_PART, t % PER_PART
            for h in (0, 1):
                mine[step % 4, part, h, i] = keep[:, h * HALF:h * HALF + HALF]
                part_send[step, part, h, i] = give[:, h * HALF:h * HALF + HALF]

            @pl.when(t == 4 + 3 * (step >= 6).astype(jnp.int32))
            def _():
                lax.fori_loop(pick(step, PASSED), pick(step, PASSED[1:]), lambda s, carry: pass_on_all(s), 0)

            @pl.when((t == 8) & (step >= 6))
            def _():
                lax.fori_loop(pick(step, JOINED), pick(step, JOINED[1:]), lambda s, carry: join_y_all(s), 0)

            @pl.when(t == 3)
            def _():
                send_part(step, 0)

            @pl.when((t == 5) | (t == 8))
            def _():
                join_cores(step, t // 4 - 1)

            @pl.when(t == 6)
            def _():
                send_part(step, 1)

            return carry

        lax.fori_loop(0, TILES, tile_body, 0)
        send_part(step, 2)
        join_cores(step, 2)

        return carry

    lax.fori_loop(0, STEPS, step_body, 0)
    pass_on_all(7)
    join_y_all(6)
    lax.fori_loop(0, 6, lambda s, carry: announce_all(s), 0)

    scale = ADAPTER_SCALE / (16 * ROWS)

    spread_end(la, la_ss, la_rs)
    for s in range(STEPS):
        for kind in (0, 1):
            flip, dz = ORDER[kind][s]
            n = ((xh + flip) % 2) * 4 + ring(z, dz)
            la_t[pl.ds((s * 2 + kind) * ROWS, ROWS), :] = la[n * 2 + kind]
    lg_t[...] = la_t[...].T

    def gb_body(t, carry):
        cols = pl.ds(pl.multiple_of(t * TILE, TILE), TILE)
        tokens = g[:, :, cols].reshape(16 * ROWS, TILE)
        gb_ref[:, cols] = scale * dot_nn(lg_t[...], tokens)
        return carry

    lax.fori_loop(0, F_LOCAL // TILE, gb_body, 0)

    announce_all(6)
    join_y_all(7)
    announce_all(7)
    for i, (dx, k) in enumerate(CHIPS):
        other = wide_id((xl + dx) % 2, ring(y, k), c)
        blk = lg.at[other]
        arrived(blk, lg_rs.at[other], lg_ss.at[0])
        send(blk, blk, lg_ss.at[8 + i], lg_rs.at[other], partner)

    spread_end(xs_all, in_ss, in_rs)
    spread_end(lg, lg_ss, lg_rs)
    lg_t[...] = lg[...].reshape(16 * ROWS, R).T

    def ga_body(t, carry):
        cols = pl.ds(pl.multiple_of(t * TILE, TILE), TILE)
        tokens = xs_all[:, :, cols].reshape(16 * ROWS, TILE)
        ga_ref[:, cols] = scale * dot_nn(lg_t[...], tokens)
        return carry

    lax.fori_loop(0, D_LOCAL // TILE, ga_body, 0)

    low_rows = lg[wi]

    def ig_body(t, carry):
        cols = pl.ds(pl.multiple_of(t * TILE, TILE), TILE)
        part, i = (t + 1) // PER_PART, (t + 1) % PER_PART
        base = jnp.concatenate([own_total(part, 0, i), own_total(part, 1, i)], axis=1)
        ig_ref[:, cols] = (base + ADAPTER_SCALE * dot_nt(low_rows, a[cols, :])).astype(BF16)
        return carry

    for part in range(PARTS):
        if part:
            arrived(x_recv.at[part], x_rs.at[part], x_ss.at[part])
        lax.fori_loop(max(part * PER_PART - 1, 0), (part + 1) * PER_PART - 1, ig_body, 0)

    for sem, cut in enumerate(g_sends):
        sent(g_slot((0, 0), None)[0] if cut is None else g.at[0, pl.ds(*CUTS[cut])], g_ss.at[sem], g_rs.at[0])
    for k in range(3):
        sent(lp.at[0], l1_ss.at[k], l1_rs.at[k])
        sent(lo.at[0], l3_ss.at[k], l3_rs.at[k])
    sent(l2s, l2_ss, l2_rs)
    spread_sent(xs_all, in_ss, in_rs)
    spread_sent(la, la_ss, la_rs)
    spread_sent(lg, lg_ss, lg_rs)

    def drain(step, carry):
        xl_n, y_n = owner(step)
        for part in range(PARTS):
            sent(part_send.at[step, part], c_ss.at[step, part], c_rs.at[step, part])

            @pl.when(y_n != y)
            def _(part=part):
                for h in (0, 1):
                    sent(part_recv.at[step, part, h], y_ss.at[step, part, h], y_rs.at[0, 0, part, h])

        return carry

    lax.fori_loop(0, STEPS, drain, 0)
    for part in range(PARTS):
        sent(x_send.at[part], x_ss.at[part], x_rs.at[part])


def shards(inputs, grad_out, w_base, adapter_down_matrix, b_factor):
    dma = pltpu.SemaphoreType.DMA
    pieces = (PARTS, 2, PER_PART, ROWS, HALF)
    scratch = [
        pltpu.VMEM((16, ROWS, F_LOCAL), BF16),
        pltpu.VMEM((R + D_LOCAL, F_LOCAL), BF16),
        pltpu.VMEM((D_LOCAL, R), BF16),
        pltpu.VMEM((16, ROWS, D_LOCAL), BF16),
        pltpu.VMEM((STEPS,) + pieces, BF16),
        pltpu.VMEM((STEPS,) + pieces, BF16),
        pltpu.VMEM((4,) + pieces, F32),
        pltpu.VMEM((2, 2, PARTS, PER_PART, ROWS, HALF), BF16),
        pltpu.VMEM((2, 2) + pieces, BF16),
        pltpu.VMEM((2,) + pieces, F32),
        pltpu.VMEM(pieces, BF16),
        pltpu.VMEM(pieces, BF16),
        pltpu.VMEM((4, 56, 128), F32),
        pltpu.VMEM((3, 56, 128), F32),
        pltpu.VMEM((56, 128), F32),
        pltpu.VMEM((56, 128), F32),
        pltpu.VMEM((4, 56, 128), F32),
        pltpu.VMEM((16, ROWS, R), BF16),
        pltpu.VMEM((16 * ROWS, R), BF16),
        pltpu.VMEM((16, ROWS, R), BF16),
        pltpu.VMEM((R, 16 * ROWS), BF16),
        dma((6,)), dma((16,)), dma((18,)), dma((STEPS, PARTS)), dma((STEPS, PARTS)),
        dma((2, 2, PARTS)), dma((STEPS, PARTS, 2)), dma((2, 2, PARTS, 2)), dma((PARTS,)), dma((PARTS,)),
        dma((15,)), dma((16,)), dma((15,)), dma((16,)), dma((15,)), dma((16,)),
        dma((3,)), dma((3,)), dma(()), dma(()), dma((3,)), dma((4,)),
    ]
    any_spec = pl.BlockSpec(memory_space=pl.ANY)
    vmem_spec = pl.BlockSpec(memory_space=pltpu.VMEM)
    input_gradient, grad_a, grad_b = pl.pallas_call(
        kernel,
        out_shape=(
            jax.ShapeDtypeStruct((ROWS, D_LOCAL), BF16),
            jax.ShapeDtypeStruct((R, D_LOCAL), F32),
            jax.ShapeDtypeStruct((R, F_LOCAL), F32),
        ),
        in_specs=[any_spec] * 5,
        out_specs=(vmem_spec,) * 3,
        scratch_shapes=scratch,
        compiler_params=pltpu.CompilerParams(
            collective_id=0, has_side_effects=True, vmem_limit_bytes=67043328
        ),
        name="backward",
    )(inputs, grad_out, w_base, adapter_down_matrix, b_factor)
    return input_gradient, grad_a.T, grad_b


def solution(mesh):
    return jax.shard_map(
        shards,
        mesh=mesh,
        in_specs=(
            P("wide", "narrow"),
            P("narrow", "wide"),
            P("narrow", "wide"),
            P("narrow", None),
            P(None, "wide"),
        ),
        out_specs=(P("wide", "narrow"), P("narrow", None), P(None, "wide")),
        check_vma=False,
    )
```

```python
import jax
import jax.numpy as jnp
from jax import lax
from jax.experimental import pallas as pl
from jax.experimental.pallas import tpu as pltpu
from jax.sharding import PartitionSpec as P

ADAPTER_SCALE = 2.0
ROWS = 112
F_LOCAL = 3328
D_LOCAL = 2048
R = 256
TILE = 256
TILES = (R + D_LOCAL) // TILE
PARTS = 3
PER_PART = TILES // PARTS
HALF = TILE // 2
PASSED = (0, 0, 0, 1, 2, 2, 5, 6, 7)
JOINED = (0, 0, 0, 0, 0, 0, 2, 4, 6)
CHIPS = ((0, 1), (0, 3), (0, 2), (1, 0), (1, 1), (1, 3), (1, 2))
CUTS = ((0, 64), (64, 48))
STEPS = 8
MESH = pl.DeviceIdType.MESH
BF16 = jnp.bfloat16
F32 = jnp.float32

ORDER = (
    ((0, 0), (0, 1), (1, 0), (0, 3), (1, 3), (0, 2), (1, 1), (1, 2)),
    ((0, 0), (0, 3), (0, 1), (1, 0), (0, 2), (1, 1), (1, 3), (1, 2)),
)


def dot_nt(a, b):
    return lax.dot_general(a, b, (((1,), (1,)), ((), ())), preferred_element_type=F32)


def dot_nn(a, b):
    return lax.dot_general(a, b, (((1,), (0,)), ((), ())), preferred_element_type=F32)


def pick(index, values):
    if isinstance(index, int):
        return values[index]
    out = index * 0 + values[0]
    for i, value in enumerate(values[1:STEPS], 1):
        out = out + (index == i).astype(jnp.int32) * (value - values[0])
    return out


def kernel(
    x_hbm, g_hbm, w_hbm, a_hbm, b_hbm,
    ig_hbm, ga_hbm, gb_hbm,
    ig_ref, ga_ref, gb_ref,
    g, w, a, xs_all, part_send, part_recv, mine, relay, y_recv, y_own, x_send, x_recv,
    lp, l1, l2s, l2r, lo, la, la_t, lg, lg_t,
    ld_sem, out_sem, g_ss, g_rs, c_ss, c_rs, f_rs, y_ss, y_rs, x_ss, x_rs,
    in_ss, in_rs, la_ss, la_rs, lg_ss, lg_rs, l1_ss, l1_rs, l2_ss, l2_rs, l3_ss, l3_rs,
):
    wi = lax.axis_index("wide")
    ni = lax.axis_index("narrow")
    xl, y, c = wi // 8, (wi // 2) % 4, wi % 2
    xh, z = ni // 4, ni % 4

    def wide_id(xl_, y_, c_):
        return (xl_ * 4 + y_) * 2 + c_

    def ring(v, k):
        return (v + k) % 4

    def wide_dev(xl_, y_, c_):
        return (wide_id(xl_, y_, c_), ni)

    partner = wide_dev(xl, y, 1 - c)
    x_pair = wide_dev(1 - xl, y, c)
    x_cross = (wi, (1 - xh) * 4 + z)
    z_next = (wi, xh * 4 + ring(z, 1))
    z_prev = (wi, xh * 4 + ring(z, 3))

    def send(src, dst, ss, rs, dev):
        cp = pltpu.make_async_remote_copy(
            src_ref=src, dst_ref=dst, send_sem=ss, recv_sem=rs, device_id=dev, device_id_type=MESH
        )
        cp.start()
        return cp

    def arrived(dst, rs, ss):
        pltpu.make_async_remote_copy(
            src_ref=dst, dst_ref=dst, send_sem=ss, recv_sem=rs, device_id=partner, device_id_type=MESH
        ).wait_recv()

    def sent(src, ss, rs):
        pltpu.make_async_remote_copy(
            src_ref=src, dst_ref=src, send_sem=ss, recv_sem=rs, device_id=partner, device_id_type=MESH
        ).wait_send()

    loads = [
        pltpu.make_async_copy(x_hbm, xs_all.at[wi], ld_sem.at[0]),
        pltpu.make_async_copy(a_hbm, a, ld_sem.at[1]),
        pltpu.make_async_copy(g_hbm.at[pl.ds(0, ROWS)], g.at[0], ld_sem.at[2]),
        pltpu.make_async_copy(g_hbm.at[pl.ds(ROWS, ROWS)], g.at[1], ld_sem.at[3]),
        pltpu.make_async_copy(b_hbm, w.at[pl.ds(0, R)], ld_sem.at[4]),
        pltpu.make_async_copy(w_hbm, w.at[pl.ds(R, D_LOCAL)], ld_sem.at[5]),
    ]
    for cp in loads:
        cp.start()

    barrier = pltpu.get_barrier_semaphore()
    peers = [(wi, xh * 4 + ring(z, k)) for k in (1, 2, 3)] + [x_cross, partner]
    for dx in (0, 1):
        for k in range(4):
            if dx or k:
                peers.append(wide_dev(xl if dx == 0 else 1 - xl, ring(y, k), c))
    for dev in peers:
        pl.semaphore_signal(barrier, inc=1, device_id=dev, device_id_type=MESH)
    pl.semaphore_wait(barrier, len(peers))

    g_sends = []

    def g_slot(unit, cut):
        slot = unit[0] * 2 + unit[1]
        if cut is None:
            return g.at[slot], slot
        return g.at[slot, pl.ds(*CUTS[cut])], slot if cut == 0 else 16 + unit[0] - 6

    def g_send(src, dst, dev, cut=None):
        ref, sem = g_slot(dst, cut)
        if isinstance(src, tuple):
            src = g_slot(src, cut)[0]
        elif cut is not None:
            src = src.at[pl.ds(*CUTS[cut])]
        send(src, ref, g_ss.at[len(g_sends)], g_rs.at[sem], dev)
        g_sends.append(cut)

    def g_wait(step, kind, cut=None):
        ref, sem = g_slot((step, kind), cut)
        arrived(ref, g_rs.at[sem], g_ss.at[0])

    own0, own1 = g_hbm.at[pl.ds(0, ROWS)], g_hbm.at[pl.ds(ROWS, ROWS)]
    g_send(own0, (2, 0), x_cross)
    g_send(own1, (1, 1), z_next)
    g_send(own0, (1, 0), z_prev)

    def spread_own(buf, ss, rs):
        me = buf.at[wi]
        send(me, me, ss.at[0], rs.at[wi], x_pair)
        for k in (1, 3, 2):
            send(me, me, ss.at[k], rs.at[wi], wide_dev(xl, ring(y, k), c))
        send(me, me, ss.at[4], rs.at[wi], partner)

    def spread_pair(buf, ss, rs, near=True, far=True):
        other = wide_id(1 - xl, y, c)
        blk = buf.at[other]
        if near:
            arrived(blk, rs.at[other], ss.at[0])
            send(blk, blk, ss.at[8], rs.at[other], partner)
        for i, k in enumerate((1, 3, 2)):
            if near and k != 2 or far and k == 2:
                send(blk, blk, ss.at[5 + i], rs.at[other], wide_dev(xl, ring(y, k), c))

    def spread_core(buf, ss, rs, blocks=range(6)):
        for i in blocks:
            other = wide_id(xl if i < 3 else 1 - xl, ring(y, (1, 3, 2)[i % 3]), c)
            blk = buf.at[other]
            arrived(blk, rs.at[other], ss.at[0])
            send(blk, blk, ss.at[9 + i], rs.at[other], partner)

    def spread_end(buf, ss, rs):
        for xl_ in (0, 1):
            for y_ in range(4):
                other = wide_id(xl_, y_, 1 - c)
                arrived(buf.at[other], rs.at[other], ss.at[0])

    loads[0].wait()
    spread_own(xs_all, in_ss, in_rs)

    loads[1].wait()
    low = dot_nn(xs_all[wi], a[...])
    for rh in (0, 1):
        for ch in (0, 1):
            lp[rh * 2 + ch] = low[rh * 56:rh * 56 + 56, ch * 128:ch * 128 + 128]

    def low_stage1():
        for k in (1, 3, 2):
            q = ring(z, k)
            send(lp.at[q], l1.at[3 - k], l1_ss.at[k - 1], l1_rs.at[3 - k], (wi, xh * 4 + q))

    def low_stage2():
        for k in range(3):
            arrived(l1.at[k], l1_rs.at[k], l1_ss.at[k])
        l2s[...] = lp[z] + l1[0] + l1[1] + l1[2]
        send(l2s, l2r, l2_ss, l2_rs, x_cross)

    def low_stage3():
        arrived(l2r, l2_rs, l2_ss)
        lo[z] = l2s[...] + l2r[...]
        for k in (1, 3, 2):
            send(lo.at[z], lo.at[z], l3_ss.at[k - 1], l3_rs.at[z], (wi, xh * 4 + ring(z, k)))

    def low_stage4():
        for k in (1, 2, 3):
            q = ring(z, k)
            arrived(lo.at[q], l3_rs.at[q], l3_ss.at[k - 1])
        top = jnp.concatenate([lo[0], lo[1]], axis=1)
        bottom = jnp.concatenate([lo[2], lo[3]], axis=1)
        la[wi] = jnp.concatenate([top, bottom], axis=0).astype(BF16)
        spread_own(la, la_ss, la_rs)

    low_stage1()
    g_send(own0, (3, 0), z_next)
    g_send(own1, (2, 1), z_prev)

    for cp in loads[2:]:
        cp.wait()

    def owner(step):
        flip, dz = (
            pick(step, [t[i] for t in ORDER[0]]) * (1 - c) + pick(step, [t[i] for t in ORDER[1]]) * c
            for i in (0, 1)
        )
        return (xh + flip) % 2, ring(z, dz)

    def send_part(step, part):
        send(part_send.at[step, part], part_recv.at[step, part],
             c_ss.at[step, part], c_rs.at[step, part], partner)

    def join_cores(step, part):
        xl_n, y_n = owner(step)
        d = (y - y_n + 4) % 4
        arrived(part_recv.at[step, part], c_rs.at[step, part], c_ss.at[step, part])

        def total(h, i):
            return mine[step % 4, part, h, i] + part_recv[step, part, h, i].astype(F32)

        @pl.when(d == 0)
        def _():
            for h in (0, 1):
                for i in range(PER_PART):
                    y_own[xl_n, part, h, i] = total(h, i)

        @pl.when(d == 2)
        def _():
            for h in (0, 1):
                for i in range(PER_PART):
                    part_recv[step, part, h, i] = total(h, i).astype(BF16)
            for h, k in ((0, 3), (1, 1)):
                send(part_recv.at[step, part, h], relay.at[h, xl_n, part], y_ss.at[step, part, h],
                     f_rs.at[h, xl_n, part], wide_dev(xl, ring(y, k), c))

        @pl.when(d % 2 == 1)
        def _():
            late = d // 2
            for i in range(PER_PART):
                mine[step % 4, part, late, i] = total(late, i)
                part_recv[step, part, 1 - late, i] = total(1 - late, i).astype(BF16)
            send(part_recv.at[step, part, 1 - late], y_recv.at[late, xl_n, part, 1 - late],
                 y_ss.at[step, part, 1 - late], y_rs.at[late, xl_n, part, 1 - late], wide_dev(xl, y_n, c))

    def pass_on(step, part):
        xl_n, y_n = owner(step)
        d = (y - y_n + 4) % 4

        @pl.when(d % 2 == 1)
        def _():
            late = d // 2
            arrived(relay.at[late, xl_n, part], f_rs.at[late, xl_n, part], x_ss.at[part])
            for i in range(PER_PART):
                part_recv[step, part, late, i] = (
                    mine[step % 4, part, late, i] + relay[late, xl_n, part, i].astype(F32)
                ).astype(BF16)
            send(part_recv.at[step, part, late], y_recv.at[late, xl_n, part, late],
                 y_ss.at[step, part, late], y_rs.at[late, xl_n, part, late], wide_dev(xl, y_n, c))

    def join_y(step, part):
        xl_n, y_n = owner(step)

        @pl.when(y_n == y)
        def _():
            for r in (0, 1):
                for h in (0, 1):
                    arrived(y_recv.at[r, xl_n, part, h], y_rs.at[r, xl_n, part, h], x_ss.at[part])

            def total(h, i):
                return (y_own[xl_n, part, h, i] + y_recv[0, xl_n, part, h, i].astype(F32)
                        + y_recv[1, xl_n, part, h, i].astype(F32))

            @pl.when(xl_n == xl)
            def _():
                for h in (0, 1):
                    for i in range(PER_PART):
                        y_own[xl_n, part, h, i] = total(h, i)

            @pl.when(xl_n != xl)
            def _():
                for h in (0, 1):
                    for i in range(PER_PART):
                        x_send[part, h, i] = total(h, i).astype(BF16)
                send(x_send.at[part], x_recv.at[part], x_ss.at[part], x_rs.at[part], x_pair)

    def over_parts(do, step):
        def body(part, carry):
            do(step, part)
            return carry

        return lax.fori_loop(0, PARTS, body, 0)

    def pass_on_all(step):
        return over_parts(pass_on, step)

    def join_y_all(step):
        return over_parts(join_y, step)

    def own_total(part, h, i):
        return y_own[xl, part, h, i] + x_recv[part, h, i].astype(F32)

    def announce_all(step):
        xl_n, y_n = owner(step)

        @pl.when((xl_n == xl) & (y_n == y))
        def _():
            arrived(x_recv.at[0], x_rs.at[0], x_ss.at[0])
            lg[wi] = jnp.concatenate([own_total(0, 0, 0), own_total(0, 1, 0)], axis=1).astype(BF16)
            me = lg.at[wi]
            send(me, me, lg_ss.at[0], lg_rs.at[wi], partner)
            for i, (dx, k) in enumerate(CHIPS):
                send(me, me, lg_ss.at[1 + i], lg_rs.at[wi], wide_dev((xl + dx) % 2, ring(y, k), c))

        return 0

    def drain(step, carry):
        xl_n, y_n = owner(step)
        for part in range(PARTS):
            sent(part_send.at[step, part], c_ss.at[step, part], c_rs.at[step, part])

        @pl.when(y_n != y)
        def _():
            for part in range(PARTS):
                for h in (0, 1):
                    sent(part_recv.at[step, part, h], y_ss.at[step, part, h], y_rs.at[0, 0, part, h])

        return carry

    def drain_first():
        for sem in range(5):
            sent(g.at[0], g_ss.at[sem], g_rs.at[0])
        for k in range(3):
            sent(lp.at[0], l1_ss.at[k], l1_rs.at[k])
            sent(lo.at[0], l3_ss.at[k], l3_rs.at[k])
        sent(l2s, l2_ss, l2_rs)
        for i in range(5):
            sent(xs_all.at[wi], in_ss.at[i], in_rs.at[wi])
        lax.fori_loop(0, 2, drain, 0)

    def drain_most():
        for sem, cut in enumerate(g_sends):
            if sem >= 5:
                sent(g.at[0] if cut is None else g.at[0, pl.ds(*CUTS[cut])], g_ss.at[sem], g_rs.at[0])
        for i in range(15):
            sent(la.at[wi], la_ss.at[i], la_rs.at[wi])
            if i >= 5:
                sent(xs_all.at[wi], in_ss.at[i], in_rs.at[wi])
        lax.fori_loop(2, 6, drain, 0)

    def before(step):
        if step == 1:
            g_wait(1, 0)
            low_stage2()
            g_send(g_hbm.at[pl.ds(ROWS, ROWS)], (3, 1), x_cross)
            g_send((1, 0), (6, 0), x_cross)
            g_wait(1, 1)
            g_send(g.at[3], (6, 1), x_cross, 0)
            g_send(g.at[3], (6, 1), x_cross, 1)
        if step == 2:
            g_wait(2, 0)
            g_send((2, 0), (4, 0), z_next)
            low_stage3()
            g_wait(2, 1)
            g_send((2, 1), (4, 1), z_prev)
            g_wait(3, 0)
            g_send((3, 0), (5, 0), z_next)
            spread_pair(xs_all, in_ss, in_rs, far=False)
        if step == 3:
            g_wait(3, 1)
            g_send((3, 1), (5, 1), z_prev)
            spread_pair(xs_all, in_ss, in_rs, near=False)
        if step == 4:
            g_wait(4, 1)
            g_wait(4, 0)
            low_stage4()
        if step == 5:
            g_wait(6, 0)
            g_send((6, 0), (7, 0), z_prev)
            spread_core(xs_all, in_ss, in_rs, range(3))
            join_y_all(0)
            join_y_all(1)
            drain_first()
            g_wait(6, 1, 0)
            g_send((6, 1), (7, 1), z_next, 0)
            g_wait(5, 0)
            g_wait(5, 1)
        if step == 6:
            spread_core(xs_all, in_ss, in_rs, range(3, 6))
            g_wait(6, 1, 1)
            g_send((6, 1), (7, 1), z_next, 1)
            spread_pair(la, la_ss, la_rs)
        if step == 7:
            spread_core(la, la_ss, la_rs)
            g_wait(7, 0)
            g_wait(7, 1, 0)
            g_wait(7, 1, 1)

    def step_body(step, carry):
        for k in range(1, STEPS):
            @pl.when(step == k)
            def _(k=k):
                before(k)

        def tile_body(t, carry):
            rows = g[pl.ds(step * 2, 2)].reshape(2 * ROWS, F_LOCAL)
            cols = w[pl.ds(pl.multiple_of(t * TILE, TILE), TILE), :]
            acc = dot_nt(rows, cols)
            top, bottom = acc[:ROWS], acc[ROWS:]
            keep, give = jnp.where(c == 0, top, bottom), jnp.where(c == 0, bottom, top).astype(BF16)
            part, i = t // PER_PART, t % PER_PART
            for h in (0, 1):
                mine[step % 4, part, h, i] = keep[:, h * HALF:h * HALF + HALF]
                part_send[step, part, h, i] = give[:, h * HALF:h * HALF + HALF]

            @pl.when(t == 4 + 3 * (step >= 6).astype(jnp.int32))
            def _():
                lax.fori_loop(pick(step, PASSED), pick(step, PASSED[1:]), lambda s, carry: pass_on_all(s), 0)

            @pl.when((t == 8) & (step >= 6))
            def _():
                lax.fori_loop(pick(step, JOINED), pick(step, JOINED[1:]), lambda s, carry: join_y_all(s), 0)

            @pl.when(t == 3)
            def _():
                send_part(step, 0)

            @pl.when((t == 5) | (t == 8))
            def _():
                join_cores(step, t // 4 - 1)

            @pl.when(t == 6)
            def _():
                send_part(step, 1)

            return carry

        lax.fori_loop(0, TILES, tile_body, 0)
        send_part(step, 2)
        join_cores(step, 2)

        return carry

    lax.fori_loop(0, STEPS, step_body, 0)
    pass_on_all(7)
    join_y_all(6)
    lax.fori_loop(0, 6, lambda s, carry: announce_all(s), 0)

    scale = ADAPTER_SCALE / (16 * ROWS)

    spread_end(la, la_ss, la_rs)
    for s in range(STEPS):
        for kind in (0, 1):
            flip, dz = ORDER[kind][s]
            n = ((xh + flip) % 2) * 4 + ring(z, dz)
            la_t[pl.ds((s * 2 + kind) * ROWS, ROWS), :] = la[n * 2 + kind]
    lg_t[...] = la_t[...].T

    def gb_body(t, carry):
        cols = pl.ds(pl.multiple_of(t * TILE, TILE), TILE)
        tokens = g[:, :, cols].reshape(16 * ROWS, TILE)
        gb_ref[:, cols] = scale * dot_nn(lg_t[...], tokens)
        return carry

    lax.fori_loop(0, F_LOCAL // TILE, gb_body, 0)
    gb_out = pltpu.make_async_copy(gb_ref, gb_hbm, out_sem.at[0])
    gb_out.start()

    announce_all(6)
    drain_most()
    join_y_all(7)
    announce_all(7)
    for i, (dx, k) in enumerate(CHIPS):
        other = wide_id((xl + dx) % 2, ring(y, k), c)
        blk = lg.at[other]
        arrived(blk, lg_rs.at[other], lg_ss.at[0])
        send(blk, blk, lg_ss.at[8 + i], lg_rs.at[other], partner)

    spread_end(xs_all, in_ss, in_rs)
    spread_end(lg, lg_ss, lg_rs)
    lg_t[...] = lg[...].reshape(16 * ROWS, R).T

    def ga_body(t, carry):
        cols = pl.ds(pl.multiple_of(t * TILE, TILE), TILE)
        tokens = xs_all[:, :, cols].reshape(16 * ROWS, TILE)
        ga_ref[t] = scale * dot_nn(lg_t[...], tokens)
        pltpu.make_async_copy(ga_ref.at[t], ga_hbm.at[t], out_sem.at[2 + t]).start()
        return carry

    lax.fori_loop(0, D_LOCAL // TILE, ga_body, 0)

    low_rows = lg[wi]

    def ig_body(t, carry):
        cols = pl.ds(pl.multiple_of(t * TILE, TILE), TILE)
        part, i = (t + 1) // PER_PART, (t + 1) % PER_PART
        base = jnp.concatenate([own_total(part, 0, i), own_total(part, 1, i)], axis=1)
        ig_ref[:, cols] = (base + ADAPTER_SCALE * dot_nt(low_rows, a[cols, :])).astype(BF16)
        return carry

    for part in range(PARTS):
        if part:
            arrived(x_recv.at[part], x_rs.at[part], x_ss.at[part])
        lax.fori_loop(max(part * PER_PART - 1, 0), (part + 1) * PER_PART - 1, ig_body, 0)

    ig_out = pltpu.make_async_copy(ig_ref, ig_hbm, out_sem.at[1])
    ig_out.start()

    for i in range(15):
        sent(lg.at[wi], lg_ss.at[i], lg_rs.at[wi])
    lax.fori_loop(6, STEPS, drain, 0)
    gb_out.wait()
    for t in range(D_LOCAL // TILE):
        pltpu.make_async_copy(ga_ref.at[t], ga_hbm.at[t], out_sem.at[2 + t]).wait()
    ig_out.wait()
    for part in range(PARTS):
        sent(x_send.at[part], x_ss.at[part], x_rs.at[part])


def results(ig, ga, gb, ig_out, ga_out, gb_out, ig_buf, ga_buf, gat_buf, gb_buf, in_sem, out_sem):
    blocks = D_LOCAL // TILE
    rows = R // 4
    pairs = [(ga.at[t], ga_buf.at[t], gat_buf.at[t], ga_out.at[pl.ds(t * TILE, TILE)]) for t in range(blocks)]
    for i in range(4):
        cut = pl.ds(i * rows, rows)
        pairs.append((gb.at[cut], gb_buf.at[cut], gb_buf.at[cut], gb_out.at[cut]))
    pairs.append((ig, ig_buf, ig_buf, ig_out))
    loads = [pltpu.make_async_copy(p[0], p[1], in_sem.at[i]) for i, p in enumerate(pairs)]
    stores = [pltpu.make_async_copy(p[2], p[3], out_sem.at[i]) for i, p in enumerate(pairs)]
    for cp in loads:
        cp.start()
    for i in range(len(pairs)):
        loads[i].wait()
        if i < blocks:
            gat_buf[i] = ga_buf[i].T
        stores[i].start()
    for cp in stores:
        cp.wait()


def shards(inputs, grad_out, w_base, adapter_down_matrix, b_factor):
    dma = pltpu.SemaphoreType.DMA
    pieces = (PARTS, 2, PER_PART, ROWS, HALF)
    scratch = [
        pltpu.VMEM((ROWS, D_LOCAL), BF16),
        pltpu.VMEM((D_LOCAL // TILE, R, TILE), F32),
        pltpu.VMEM((R, F_LOCAL), F32),
        pltpu.VMEM((16, ROWS, F_LOCAL), BF16),
        pltpu.VMEM((R + D_LOCAL, F_LOCAL), BF16),
        pltpu.VMEM((D_LOCAL, R), BF16),
        pltpu.VMEM((16, ROWS, D_LOCAL), BF16),
        pltpu.VMEM((STEPS,) + pieces, BF16),
        pltpu.VMEM((STEPS,) + pieces, BF16),
        pltpu.VMEM((4,) + pieces, F32),
        pltpu.VMEM((2, 2, PARTS, PER_PART, ROWS, HALF), BF16),
        pltpu.VMEM((2, 2) + pieces, BF16),
        pltpu.VMEM((2,) + pieces, F32),
        pltpu.VMEM(pieces, BF16),
        pltpu.VMEM(pieces, BF16),
        pltpu.VMEM((4, 56, 128), F32),
        pltpu.VMEM((3, 56, 128), F32),
        pltpu.VMEM((56, 128), F32),
        pltpu.VMEM((56, 128), F32),
        pltpu.VMEM((4, 56, 128), F32),
        pltpu.VMEM((16, ROWS, R), BF16),
        pltpu.VMEM((16 * ROWS, R), BF16),
        pltpu.VMEM((16, ROWS, R), BF16),
        pltpu.VMEM((R, 16 * ROWS), BF16),
        dma((6,)), dma((10,)), dma((16,)), dma((18,)), dma((STEPS, PARTS)), dma((STEPS, PARTS)),
        dma((2, 2, PARTS)), dma((STEPS, PARTS, 2)), dma((2, 2, PARTS, 2)), dma((PARTS,)), dma((PARTS,)),
        dma((15,)), dma((16,)), dma((15,)), dma((16,)), dma((15,)), dma((16,)),
        dma((3,)), dma((3,)), dma(()), dma(()), dma((3,)), dma((4,)),
    ]
    any_spec = pl.BlockSpec(memory_space=pl.ANY)
    input_gradient, grad_a, grad_b = pl.pallas_call(
        kernel,
        out_shape=(
            jax.ShapeDtypeStruct((ROWS, D_LOCAL), BF16),
            jax.ShapeDtypeStruct((D_LOCAL // TILE, R, TILE), F32),
            jax.ShapeDtypeStruct((R, F_LOCAL), F32),
        ),
        in_specs=[any_spec] * 5,
        out_specs=(any_spec,) * 3,
        scratch_shapes=scratch,
        compiler_params=pltpu.CompilerParams(
            collective_id=0, has_side_effects=True, vmem_limit_bytes=67043328
        ),
        name="backward",
    )(inputs, grad_out, w_base, adapter_down_matrix, b_factor)
    blocks = D_LOCAL // TILE
    return pl.pallas_call(
        results,
        out_shape=(
            jax.ShapeDtypeStruct((ROWS, D_LOCAL), BF16),
            jax.ShapeDtypeStruct((D_LOCAL, R), F32),
            jax.ShapeDtypeStruct((R, F_LOCAL), F32),
        ),
        in_specs=[any_spec] * 3,
        out_specs=(any_spec,) * 3,
        scratch_shapes=[
            pltpu.VMEM((ROWS, D_LOCAL), BF16),
            pltpu.VMEM((blocks, R, TILE), F32),
            pltpu.VMEM((blocks, TILE, R), F32),
            pltpu.VMEM((R, F_LOCAL), F32),
            dma((blocks + 5,)),
            dma((blocks + 5,)),
        ],
        name="results",
    )(input_gradient, grad_a, grad_b)


def solution(mesh):
    return jax.shard_map(
        shards,
        mesh=mesh,
        in_specs=(
            P("wide", "narrow"),
            P("narrow", "wide"),
            P("narrow", "wide"),
            P("narrow", None),
            P(None, "wide"),
        ),
        out_specs=(P("wide", "narrow"), P("narrow", None), P(None, "wide")),
        check_vma=False,
    )
```

```python
import jax
import jax.numpy as jnp
from jax import lax
from jax.experimental import pallas as pl
from jax.experimental.pallas import tpu as pltpu
from jax.sharding import PartitionSpec as P

ADAPTER_SCALE = 2.0
ROWS = 112
F_LOCAL = 3328
D_LOCAL = 2048
R = 256
TILE = 256
TILES = (R + D_LOCAL) // TILE
PARTS = 3
PER_PART = TILES // PARTS
HALF = TILE // 2
PASSED = (0, 0, 0, 1, 2, 2, 5, 6, 7)
JOINED = (0, 0, 0, 0, 0, 0, 2, 4, 6)
CHIPS = ((0, 1), (0, 3), (0, 2), (1, 0), (1, 1), (1, 3), (1, 2))
CUTS = ((0, 64), (64, 48))
STEPS = 8
MESH = pl.DeviceIdType.MESH
BF16 = jnp.bfloat16
F32 = jnp.float32

ORDER = (
    ((0, 0), (0, 1), (1, 0), (0, 3), (1, 3), (0, 2), (1, 1), (1, 2)),
    ((0, 0), (0, 3), (0, 1), (1, 0), (0, 2), (1, 1), (1, 3), (1, 2)),
)


def dot_nt(a, b):
    return lax.dot_general(a, b, (((1,), (1,)), ((), ())), preferred_element_type=F32)


def dot_nn(a, b):
    return lax.dot_general(a, b, (((1,), (0,)), ((), ())), preferred_element_type=F32)


def pick(index, values):
    if isinstance(index, int):
        return values[index]
    out = index * 0 + values[0]
    for i, value in enumerate(values[1:STEPS], 1):
        out = out + (index == i).astype(jnp.int32) * (value - values[0])
    return out


def kernel(
    x_hbm, g_hbm, w_hbm, a_hbm, b_hbm,
    ig_hbm, ga_hbm, gb_hbm,
    ig_ref, ga_ref, gb_ref,
    g, w, a, xs_all, part_send, part_recv, mine, relay, y_recv, y_own, x_send, x_recv,
    lp, l1, l2s, l2r, lo, la, la_t, lg, lg_t,
    ld_sem, out_sem, g_ss, g_rs, c_ss, c_rs, f_rs, y_ss, y_rs, x_ss, x_rs,
    in_ss, in_rs, la_ss, la_rs, lg_ss, lg_rs, l1_ss, l1_rs, l2_ss, l2_rs, l3_ss, l3_rs,
):
    wi = lax.axis_index("wide")
    ni = lax.axis_index("narrow")
    xl, y, c = wi // 8, (wi // 2) % 4, wi % 2
    xh, z = ni // 4, ni % 4

    def wide_id(xl_, y_, c_):
        return (xl_ * 4 + y_) * 2 + c_

    def ring(v, k):
        return (v + k) % 4

    def wide_dev(xl_, y_, c_):
        return (wide_id(xl_, y_, c_), ni)

    partner = wide_dev(xl, y, 1 - c)
    x_pair = wide_dev(1 - xl, y, c)
    x_cross = (wi, (1 - xh) * 4 + z)
    z_next = (wi, xh * 4 + ring(z, 1))
    z_prev = (wi, xh * 4 + ring(z, 3))

    def send(src, dst, ss, rs, dev):
        cp = pltpu.make_async_remote_copy(
            src_ref=src, dst_ref=dst, send_sem=ss, recv_sem=rs, device_id=dev, device_id_type=MESH
        )
        cp.start()
        return cp

    def arrived(dst, rs, ss):
        pltpu.make_async_remote_copy(
            src_ref=dst, dst_ref=dst, send_sem=ss, recv_sem=rs, device_id=partner, device_id_type=MESH
        ).wait_recv()

    def sent(src, ss, rs):
        pltpu.make_async_remote_copy(
            src_ref=src, dst_ref=src, send_sem=ss, recv_sem=rs, device_id=partner, device_id_type=MESH
        ).wait_send()

    loads = [
        pltpu.make_async_copy(x_hbm, xs_all.at[wi], ld_sem.at[0]),
        pltpu.make_async_copy(a_hbm, a, ld_sem.at[1]),
        pltpu.make_async_copy(g_hbm.at[pl.ds(0, ROWS)], g.at[0], ld_sem.at[2]),
        pltpu.make_async_copy(g_hbm.at[pl.ds(ROWS, ROWS)], g.at[1], ld_sem.at[3]),
        pltpu.make_async_copy(b_hbm, w.at[pl.ds(0, R)], ld_sem.at[4]),
        pltpu.make_async_copy(w_hbm, w.at[pl.ds(R, D_LOCAL)], ld_sem.at[5]),
    ]
    for cp in loads:
        cp.start()

    barrier = pltpu.get_barrier_semaphore()
    peers = [(wi, xh * 4 + ring(z, k)) for k in (1, 2, 3)] + [x_cross, partner]
    for dx in (0, 1):
        for k in range(4):
            if dx or k:
                peers.append(wide_dev(xl if dx == 0 else 1 - xl, ring(y, k), c))
    for dev in peers:
        pl.semaphore_signal(barrier, inc=1, device_id=dev, device_id_type=MESH)
    pl.semaphore_wait(barrier, len(peers))

    g_sends = []

    def g_slot(unit, cut):
        slot = unit[0] * 2 + unit[1]
        if cut is None:
            return g.at[slot], slot
        return g.at[slot, pl.ds(*CUTS[cut])], slot if cut == 0 else 16 + unit[0] - 6

    def g_send(src, dst, dev, cut=None):
        ref, sem = g_slot(dst, cut)
        if isinstance(src, tuple):
            src = g_slot(src, cut)[0]
        elif cut is not None:
            src = src.at[pl.ds(*CUTS[cut])]
        send(src, ref, g_ss.at[len(g_sends)], g_rs.at[sem], dev)
        g_sends.append(cut)

    def g_wait(step, kind, cut=None):
        ref, sem = g_slot((step, kind), cut)
        arrived(ref, g_rs.at[sem], g_ss.at[0])

    own0, own1 = g_hbm.at[pl.ds(0, ROWS)], g_hbm.at[pl.ds(ROWS, ROWS)]
    g_send(own0, (2, 0), x_cross)
    g_send(own1, (1, 1), z_next)
    g_send(own0, (1, 0), z_prev)

    def spread_own(buf, ss, rs):
        me = buf.at[wi]
        send(me, me, ss.at[0], rs.at[wi], x_pair)
        for k in (1, 3, 2):
            send(me, me, ss.at[k], rs.at[wi], wide_dev(xl, ring(y, k), c))
        send(me, me, ss.at[4], rs.at[wi], partner)

    def spread_pair(buf, ss, rs, near=True, far=True):
        other = wide_id(1 - xl, y, c)
        blk = buf.at[other]
        if near:
            arrived(blk, rs.at[other], ss.at[0])
            send(blk, blk, ss.at[8], rs.at[other], partner)
        for i, k in enumerate((1, 3, 2)):
            if near and k != 2 or far and k == 2:
                send(blk, blk, ss.at[5 + i], rs.at[other], wide_dev(xl, ring(y, k), c))

    def spread_core(buf, ss, rs, blocks=range(6)):
        for i in blocks:
            other = wide_id(xl if i < 3 else 1 - xl, ring(y, (1, 3, 2)[i % 3]), c)
            blk = buf.at[other]
            arrived(blk, rs.at[other], ss.at[0])
            send(blk, blk, ss.at[9 + i], rs.at[other], partner)

    def spread_end(buf, ss, rs):
        for xl_ in (0, 1):
            for y_ in range(4):
                other = wide_id(xl_, y_, 1 - c)
                arrived(buf.at[other], rs.at[other], ss.at[0])

    loads[0].wait()
    spread_own(xs_all, in_ss, in_rs)

    loads[1].wait()
    low = dot_nn(xs_all[wi], a[...])
    for rh in (0, 1):
        for ch in (0, 1):
            lp[rh * 2 + ch] = low[rh * 56:rh * 56 + 56, ch * 128:ch * 128 + 128]

    def low_stage1():
        for k in (1, 3, 2):
            q = ring(z, k)
            send(lp.at[q], l1.at[3 - k], l1_ss.at[k - 1], l1_rs.at[3 - k], (wi, xh * 4 + q))

    def low_stage2():
        for k in range(3):
            arrived(l1.at[k], l1_rs.at[k], l1_ss.at[k])
        l2s[...] = lp[z] + l1[0] + l1[1] + l1[2]
        send(l2s, l2r, l2_ss, l2_rs, x_cross)

    def low_stage3():
        arrived(l2r, l2_rs, l2_ss)
        lo[z] = l2s[...] + l2r[...]
        for k in (1, 3, 2):
            send(lo.at[z], lo.at[z], l3_ss.at[k - 1], l3_rs.at[z], (wi, xh * 4 + ring(z, k)))

    def low_stage4():
        for k in (1, 2, 3):
            q = ring(z, k)
            arrived(lo.at[q], l3_rs.at[q], l3_ss.at[k - 1])
        top = jnp.concatenate([lo[0], lo[1]], axis=1)
        bottom = jnp.concatenate([lo[2], lo[3]], axis=1)
        la[wi] = jnp.concatenate([top, bottom], axis=0).astype(BF16)
        spread_own(la, la_ss, la_rs)

    low_stage1()
    g_send(own0, (3, 0), z_next)
    g_send(own1, (2, 1), z_prev)

    for cp in loads[2:]:
        cp.wait()

    def owner(step):
        flip, dz = (
            pick(step, [t[i] for t in ORDER[0]]) * (1 - c) + pick(step, [t[i] for t in ORDER[1]]) * c
            for i in (0, 1)
        )
        return (xh + flip) % 2, ring(z, dz)

    def send_part(step, part):
        send(part_send.at[step, part], part_recv.at[step, part],
             c_ss.at[step, part], c_rs.at[step, part], partner)

    def join_cores(step, part):
        xl_n, y_n = owner(step)
        d = (y - y_n + 4) % 4
        arrived(part_recv.at[step, part], c_rs.at[step, part], c_ss.at[step, part])

        def total(h, i):
            return mine[step % 4, part, h, i] + part_recv[step, part, h, i].astype(F32)

        @pl.when(d == 0)
        def _():
            for h in (0, 1):
                for i in range(PER_PART):
                    y_own[xl_n, part, h, i] = total(h, i)

        @pl.when(d == 2)
        def _():
            for h in (0, 1):
                for i in range(PER_PART):
                    part_recv[step, part, h, i] = total(h, i).astype(BF16)
            for h, k in ((0, 3), (1, 1)):
                send(part_recv.at[step, part, h], relay.at[h, xl_n, part], y_ss.at[step, part, h],
                     f_rs.at[h, xl_n, part], wide_dev(xl, ring(y, k), c))

        @pl.when(d % 2 == 1)
        def _():
            late = d // 2
            for i in range(PER_PART):
                mine[step % 4, part, late, i] = total(late, i)
                part_recv[step, part, 1 - late, i] = total(1 - late, i).astype(BF16)
            send(part_recv.at[step, part, 1 - late], y_recv.at[late, xl_n, part, 1 - late],
                 y_ss.at[step, part, 1 - late], y_rs.at[late, xl_n, part, 1 - late], wide_dev(xl, y_n, c))

    def pass_on(step, part):
        xl_n, y_n = owner(step)
        d = (y - y_n + 4) % 4

        @pl.when(d % 2 == 1)
        def _():
            late = d // 2
            arrived(relay.at[late, xl_n, part], f_rs.at[late, xl_n, part], x_ss.at[part])
            for i in range(PER_PART):
                part_recv[step, part, late, i] = (
                    mine[step % 4, part, late, i] + relay[late, xl_n, part, i].astype(F32)
                ).astype(BF16)
            send(part_recv.at[step, part, late], y_recv.at[late, xl_n, part, late],
                 y_ss.at[step, part, late], y_rs.at[late, xl_n, part, late], wide_dev(xl, y_n, c))

    def join_y(step, part):
        xl_n, y_n = owner(step)

        @pl.when(y_n == y)
        def _():
            for r in (0, 1):
                for h in (0, 1):
                    arrived(y_recv.at[r, xl_n, part, h], y_rs.at[r, xl_n, part, h], x_ss.at[part])

            def total(h, i):
                return (y_own[xl_n, part, h, i] + y_recv[0, xl_n, part, h, i].astype(F32)
                        + y_recv[1, xl_n, part, h, i].astype(F32))

            @pl.when(xl_n == xl)
            def _():
                for h in (0, 1):
                    for i in range(PER_PART):
                        y_own[xl_n, part, h, i] = total(h, i)

            @pl.when(xl_n != xl)
            def _():
                for h in (0, 1):
                    for i in range(PER_PART):
                        x_send[part, h, i] = total(h, i).astype(BF16)
                send(x_send.at[part], x_recv.at[part], x_ss.at[part], x_rs.at[part], x_pair)

    def over_parts(do, step):
        def body(part, carry):
            do(step, part)
            return carry

        return lax.fori_loop(0, PARTS, body, 0)

    def pass_on_all(step):
        return over_parts(pass_on, step)

    def join_y_all(step):
        return over_parts(join_y, step)

    def own_total(part, h, i):
        return y_own[xl, part, h, i] + x_recv[part, h, i].astype(F32)

    def announce_all(step):
        xl_n, y_n = owner(step)

        @pl.when((xl_n == xl) & (y_n == y))
        def _():
            arrived(x_recv.at[0], x_rs.at[0], x_ss.at[0])
            lg[wi] = jnp.concatenate([own_total(0, 0, 0), own_total(0, 1, 0)], axis=1).astype(BF16)
            me = lg.at[wi]
            send(me, me, lg_ss.at[0], lg_rs.at[wi], partner)
            for i, (dx, k) in enumerate(CHIPS):
                send(me, me, lg_ss.at[1 + i], lg_rs.at[wi], wide_dev((xl + dx) % 2, ring(y, k), c))

        return 0

    def drain(step, carry):
        xl_n, y_n = owner(step)
        for part in range(PARTS):
            sent(part_send.at[step, part], c_ss.at[step, part], c_rs.at[step, part])

        @pl.when(y_n != y)
        def _():
            for part in range(PARTS):
                for h in (0, 1):
                    sent(part_recv.at[step, part, h], y_ss.at[step, part, h], y_rs.at[0, 0, part, h])

        return carry

    def drain_first():
        for sem in range(5):
            sent(g.at[0], g_ss.at[sem], g_rs.at[0])
        for k in range(3):
            sent(lp.at[0], l1_ss.at[k], l1_rs.at[k])
            sent(lo.at[0], l3_ss.at[k], l3_rs.at[k])
        sent(l2s, l2_ss, l2_rs)
        for i in range(5):
            sent(xs_all.at[wi], in_ss.at[i], in_rs.at[wi])
        lax.fori_loop(0, 2, drain, 0)

    def drain_most():
        for sem, cut in enumerate(g_sends):
            if sem >= 5:
                sent(g.at[0] if cut is None else g.at[0, pl.ds(*CUTS[cut])], g_ss.at[sem], g_rs.at[0])
        for i in range(15):
            sent(la.at[wi], la_ss.at[i], la_rs.at[wi])
            if i >= 5:
                sent(xs_all.at[wi], in_ss.at[i], in_rs.at[wi])
        lax.fori_loop(2, 6, drain, 0)

    def before(step):
        if step == 1:
            g_wait(1, 0)
            low_stage2()
            g_send(g_hbm.at[pl.ds(ROWS, ROWS)], (3, 1), x_cross)
            g_send((1, 0), (6, 0), x_cross)
            g_wait(1, 1)
            g_send(g.at[3], (6, 1), x_cross, 0)
            g_send(g.at[3], (6, 1), x_cross, 1)
        if step == 2:
            g_wait(2, 0)
            g_send((2, 0), (4, 0), z_next)
            low_stage3()
            g_wait(2, 1)
            g_send((2, 1), (4, 1), z_prev)
            g_wait(3, 0)
            g_send((3, 0), (5, 0), z_next)
            spread_pair(xs_all, in_ss, in_rs, far=False)
        if step == 3:
            g_wait(3, 1)
            g_send((3, 1), (5, 1), z_prev)
            spread_pair(xs_all, in_ss, in_rs, near=False)
        if step == 4:
            g_wait(4, 1)
            g_wait(4, 0)
            low_stage4()
        if step == 5:
            g_wait(6, 0)
            g_send((6, 0), (7, 0), z_prev)
            spread_core(xs_all, in_ss, in_rs, range(3))
            join_y_all(0)
            join_y_all(1)
            drain_first()
            g_wait(6, 1, 0)
            g_send((6, 1), (7, 1), z_next, 0)
            g_wait(5, 0)
            g_wait(5, 1)
        if step == 6:
            spread_core(xs_all, in_ss, in_rs, range(3, 6))
            g_wait(6, 1, 1)
            g_send((6, 1), (7, 1), z_next, 1)
            spread_pair(la, la_ss, la_rs)
        if step == 7:
            spread_core(la, la_ss, la_rs)
            g_wait(7, 0)
            g_wait(7, 1, 0)
            g_wait(7, 1, 1)

    def step_body(step, carry):
        for k in range(1, STEPS):
            @pl.when(step == k)
            def _(k=k):
                before(k)

        def tile_body(t, carry):
            rows = g[pl.ds(step * 2, 2)].reshape(2 * ROWS, F_LOCAL)
            cols = w[pl.ds(pl.multiple_of(t * TILE, TILE), TILE), :]
            acc = dot_nt(rows, cols)
            top, bottom = acc[:ROWS], acc[ROWS:]
            keep, give = jnp.where(c == 0, top, bottom), jnp.where(c == 0, bottom, top).astype(BF16)
            part, i = t // PER_PART, t % PER_PART
            for h in (0, 1):
                mine[step % 4, part, h, i] = keep[:, h * HALF:h * HALF + HALF]
                part_send[step, part, h, i] = give[:, h * HALF:h * HALF + HALF]

            @pl.when(t == 4 + 3 * (step >= 6).astype(jnp.int32))
            def _():
                lax.fori_loop(pick(step, PASSED), pick(step, PASSED[1:]), lambda s, carry: pass_on_all(s), 0)

            @pl.when((t == 8) & (step >= 6))
            def _():
                lax.fori_loop(pick(step, JOINED), pick(step, JOINED[1:]), lambda s, carry: join_y_all(s), 0)

            @pl.when(t == 3)
            def _():
                send_part(step, 0)

            @pl.when((t == 5) | (t == 8))
            def _():
                join_cores(step, t // 4 - 1)

            @pl.when(t == 6)
            def _():
                send_part(step, 1)

            return carry

        lax.fori_loop(0, TILES, tile_body, 0)
        send_part(step, 2)
        join_cores(step, 2)

        return carry

    lax.fori_loop(0, STEPS, step_body, 0)
    pass_on_all(7)
    join_y_all(6)
    lax.fori_loop(0, 6, lambda s, carry: announce_all(s), 0)

    scale = ADAPTER_SCALE / (16 * ROWS)

    spread_end(la, la_ss, la_rs)
    for s in range(STEPS):
        for kind in (0, 1):
            flip, dz = ORDER[kind][s]
            n = ((xh + flip) % 2) * 4 + ring(z, dz)
            la_t[pl.ds((s * 2 + kind) * ROWS, ROWS), :] = la[n * 2 + kind]
    lg_t[...] = la_t[...].T

    def gb_body(t, carry):
        cols = pl.ds(pl.multiple_of(t * TILE, TILE), TILE)
        tokens = g[:, :, cols].reshape(16 * ROWS, TILE)
        gb_ref[:, cols] = scale * dot_nn(lg_t[...], tokens)
        return carry

    lax.fori_loop(0, F_LOCAL // TILE, gb_body, 0)
    gb_out = pltpu.make_async_copy(gb_ref, gb_hbm, out_sem.at[0])
    gb_out.start()

    announce_all(6)
    drain_most()
    join_y(7, 0)
    announce_all(7)
    join_y(7, 1)
    join_y(7, 2)
    for i, (dx, k) in enumerate(CHIPS):
        other = wide_id((xl + dx) % 2, ring(y, k), c)
        blk = lg.at[other]
        arrived(blk, lg_rs.at[other], lg_ss.at[0])
        send(blk, blk, lg_ss.at[8 + i], lg_rs.at[other], partner)

    low_rows = lg[wi]

    def ig_body(t, carry):
        cols = pl.ds(pl.multiple_of(t * TILE, TILE), TILE)
        part, i = (t + 1) // PER_PART, (t + 1) % PER_PART
        base = jnp.concatenate([own_total(part, 0, i), own_total(part, 1, i)], axis=1)
        ig_ref[:, cols] = (base + ADAPTER_SCALE * dot_nt(low_rows, a[cols, :])).astype(BF16)
        return carry

    def ig_part(part):
        if part:
            arrived(x_recv.at[part], x_rs.at[part], x_ss.at[part])
        lax.fori_loop(max(part * PER_PART - 1, 0), (part + 1) * PER_PART - 1, ig_body, 0)

    ig_part(0)
    ig_part(1)

    spread_end(xs_all, in_ss, in_rs)
    spread_end(lg, lg_ss, lg_rs)
    lg_t[...] = lg[...].reshape(16 * ROWS, R).T

    def ga_body(t, carry):
        cols = pl.ds(pl.multiple_of(t * TILE, TILE), TILE)
        tokens = xs_all[:, :, cols].reshape(16 * ROWS, TILE)
        ga_ref[t] = scale * dot_nn(lg_t[...], tokens)
        pltpu.make_async_copy(ga_ref.at[t], ga_hbm.at[t], out_sem.at[2 + t]).start()
        return carry

    lax.fori_loop(0, D_LOCAL // TILE, ga_body, 0)

    ig_part(2)
    ig_out = pltpu.make_async_copy(ig_ref, ig_hbm, out_sem.at[1])
    ig_out.start()

    for i in range(15):
        sent(lg.at[wi], lg_ss.at[i], lg_rs.at[wi])
    lax.fori_loop(6, STEPS, drain, 0)
    gb_out.wait()
    for t in range(D_LOCAL // TILE):
        pltpu.make_async_copy(ga_ref.at[t], ga_hbm.at[t], out_sem.at[2 + t]).wait()
    ig_out.wait()
    for part in range(PARTS):
        sent(x_send.at[part], x_ss.at[part], x_rs.at[part])


def results(ig, ga, gb, ig_out, ga_out, gb_out, ig_buf, ga_buf, gat_buf, gb_buf, in_sem, out_sem):
    blocks = D_LOCAL // TILE
    rows = R // 4
    pairs = [(ga.at[t], ga_buf.at[t], gat_buf.at[t], ga_out.at[pl.ds(t * TILE, TILE)]) for t in range(blocks)]
    for i in range(4):
        cut = pl.ds(i * rows, rows)
        pairs.append((gb.at[cut], gb_buf.at[cut], gb_buf.at[cut], gb_out.at[cut]))
    pairs.append((ig, ig_buf, ig_buf, ig_out))
    loads = [pltpu.make_async_copy(p[0], p[1], in_sem.at[i]) for i, p in enumerate(pairs)]
    stores = [pltpu.make_async_copy(p[2], p[3], out_sem.at[i]) for i, p in enumerate(pairs)]
    for cp in loads:
        cp.start()
    for i in range(len(pairs)):
        loads[i].wait()
        if i < blocks:
            gat_buf[i] = ga_buf[i].T
        stores[i].start()
    for cp in stores:
        cp.wait()


def shards(inputs, grad_out, w_base, adapter_down_matrix, b_factor):
    dma = pltpu.SemaphoreType.DMA
    pieces = (PARTS, 2, PER_PART, ROWS, HALF)
    scratch = [
        pltpu.VMEM((ROWS, D_LOCAL), BF16),
        pltpu.VMEM((D_LOCAL // TILE, R, TILE), F32),
        pltpu.VMEM((R, F_LOCAL), F32),
        pltpu.VMEM((16, ROWS, F_LOCAL), BF16),
        pltpu.VMEM((R + D_LOCAL, F_LOCAL), BF16),
        pltpu.VMEM((D_LOCAL, R), BF16),
        pltpu.VMEM((16, ROWS, D_LOCAL), BF16),
        pltpu.VMEM((STEPS,) + pieces, BF16),
        pltpu.VMEM((STEPS,) + pieces, BF16),
        pltpu.VMEM((4,) + pieces, F32),
        pltpu.VMEM((2, 2, PARTS, PER_PART, ROWS, HALF), BF16),
        pltpu.VMEM((2, 2) + pieces, BF16),
        pltpu.VMEM((2,) + pieces, F32),
        pltpu.VMEM(pieces, BF16),
        pltpu.VMEM(pieces, BF16),
        pltpu.VMEM((4, 56, 128), F32),
        pltpu.VMEM((3, 56, 128), F32),
        pltpu.VMEM((56, 128), F32),
        pltpu.VMEM((56, 128), F32),
        pltpu.VMEM((4, 56, 128), F32),
        pltpu.VMEM((16, ROWS, R), BF16),
        pltpu.VMEM((16 * ROWS, R), BF16),
        pltpu.VMEM((16, ROWS, R), BF16),
        pltpu.VMEM((R, 16 * ROWS), BF16),
        dma((6,)), dma((10,)), dma((16,)), dma((18,)), dma((STEPS, PARTS)), dma((STEPS, PARTS)),
        dma((2, 2, PARTS)), dma((STEPS, PARTS, 2)), dma((2, 2, PARTS, 2)), dma((PARTS,)), dma((PARTS,)),
        dma((15,)), dma((16,)), dma((15,)), dma((16,)), dma((15,)), dma((16,)),
        dma((3,)), dma((3,)), dma(()), dma(()), dma((3,)), dma((4,)),
    ]
    any_spec = pl.BlockSpec(memory_space=pl.ANY)
    input_gradient, grad_a, grad_b = pl.pallas_call(
        kernel,
        out_shape=(
            jax.ShapeDtypeStruct((ROWS, D_LOCAL), BF16),
            jax.ShapeDtypeStruct((D_LOCAL // TILE, R, TILE), F32),
            jax.ShapeDtypeStruct((R, F_LOCAL), F32),
        ),
        in_specs=[any_spec] * 5,
        out_specs=(any_spec,) * 3,
        scratch_shapes=scratch,
        compiler_params=pltpu.CompilerParams(
            collective_id=0, has_side_effects=True, vmem_limit_bytes=67043328
        ),
        name="backward",
    )(inputs, grad_out, w_base, adapter_down_matrix, b_factor)
    blocks = D_LOCAL // TILE
    return pl.pallas_call(
        results,
        out_shape=(
            jax.ShapeDtypeStruct((ROWS, D_LOCAL), BF16),
            jax.ShapeDtypeStruct((D_LOCAL, R), F32),
            jax.ShapeDtypeStruct((R, F_LOCAL), F32),
        ),
        in_specs=[any_spec] * 3,
        out_specs=(any_spec,) * 3,
        scratch_shapes=[
            pltpu.VMEM((ROWS, D_LOCAL), BF16),
            pltpu.VMEM((blocks, R, TILE), F32),
            pltpu.VMEM((blocks, TILE, R), F32),
            pltpu.VMEM((R, F_LOCAL), F32),
            dma((blocks + 5,)),
            dma((blocks + 5,)),
        ],
        name="results",
    )(input_gradient, grad_a, grad_b)


def solution(mesh):
    return jax.shard_map(
        shards,
        mesh=mesh,
        in_specs=(
            P("wide", "narrow"),
            P("narrow", "wide"),
            P("narrow", "wide"),
            P("narrow", None),
            P(None, "wide"),
        ),
        out_specs=(P("wide", "narrow"), P("narrow", None), P(None, "wide")),
        check_vma=False,
    )
```

```python
import jax
import jax.numpy as jnp
from jax import lax
from jax.experimental import pallas as pl
from jax.experimental.pallas import tpu as pltpu
from jax.sharding import PartitionSpec as P

ADAPTER_SCALE = 2.0
ROWS = 112
F_LOCAL = 3328
D_LOCAL = 2048
R = 256
TILE = 256
TILES = (R + D_LOCAL) // TILE
PARTS = 3
PER_PART = TILES // PARTS
HALF = TILE // 2
PASSED = (0, 0, 0, 1, 2, 2, 5, 6, 7)
JOINED = (0, 0, 0, 0, 0, 0, 2, 4, 6)
CHIPS = ((0, 1), (0, 3), (0, 2), (1, 0), (1, 1), (1, 3), (1, 2))
CUTS = ((0, 64), (64, 48))
STEPS = 8
MESH = pl.DeviceIdType.MESH
BF16 = jnp.bfloat16
F32 = jnp.float32

ORDER = (
    ((0, 0), (0, 1), (1, 0), (0, 3), (1, 3), (0, 2), (1, 1), (1, 2)),
    ((0, 0), (0, 3), (0, 1), (1, 0), (0, 2), (1, 1), (1, 3), (1, 2)),
)


def dot_nt(a, b):
    return lax.dot_general(a, b, (((1,), (1,)), ((), ())), preferred_element_type=F32)


def dot_nn(a, b):
    return lax.dot_general(a, b, (((1,), (0,)), ((), ())), preferred_element_type=F32)


def pick(index, values):
    if isinstance(index, int):
        return values[index]
    out = index * 0 + values[0]
    for i, value in enumerate(values[1:STEPS], 1):
        out = out + (index == i).astype(jnp.int32) * (value - values[0])
    return out


def kernel(
    x_hbm, g_hbm, w_hbm, a_hbm, b_hbm,
    ig_hbm, ga_hbm, gb_hbm,
    ig_ref, ga_ref, gb_ref,
    g, w, a, xs_all, part_send, part_recv, mine, relay, y_recv, y_own, x_send, x_recv,
    lp, l1, l2s, l2r, lo, la, la_t, lg, lg_t,
    ld_sem, out_sem, ig_sem, g_ss, g_rs, c_ss, c_rs, f_rs, y_ss, y_rs, x_ss, x_rs,
    in_ss, in_rs, la_ss, la_rs, lg_ss, lg_rs, l1_ss, l1_rs, l2_ss, l2_rs, l3_ss, l3_rs,
):
    wi = lax.axis_index("wide")
    ni = lax.axis_index("narrow")
    xl, y, c = wi // 8, (wi // 2) % 4, wi % 2
    xh, z = ni // 4, ni % 4

    def wide_id(xl_, y_, c_):
        return (xl_ * 4 + y_) * 2 + c_

    def ring(v, k):
        return (v + k) % 4

    def wide_dev(xl_, y_, c_):
        return (wide_id(xl_, y_, c_), ni)

    partner = wide_dev(xl, y, 1 - c)
    x_pair = wide_dev(1 - xl, y, c)
    x_cross = (wi, (1 - xh) * 4 + z)
    z_next = (wi, xh * 4 + ring(z, 1))
    z_prev = (wi, xh * 4 + ring(z, 3))

    def send(src, dst, ss, rs, dev):
        cp = pltpu.make_async_remote_copy(
            src_ref=src, dst_ref=dst, send_sem=ss, recv_sem=rs, device_id=dev, device_id_type=MESH
        )
        cp.start()
        return cp

    def arrived(dst, rs, ss):
        pltpu.make_async_remote_copy(
            src_ref=dst, dst_ref=dst, send_sem=ss, recv_sem=rs, device_id=partner, device_id_type=MESH
        ).wait_recv()

    def sent(src, ss, rs):
        pltpu.make_async_remote_copy(
            src_ref=src, dst_ref=src, send_sem=ss, recv_sem=rs, device_id=partner, device_id_type=MESH
        ).wait_send()

    loads = [
        pltpu.make_async_copy(x_hbm, xs_all.at[wi], ld_sem.at[0]),
        pltpu.make_async_copy(a_hbm, a, ld_sem.at[1]),
        pltpu.make_async_copy(g_hbm.at[pl.ds(0, ROWS)], g.at[0], ld_sem.at[2]),
        pltpu.make_async_copy(g_hbm.at[pl.ds(ROWS, ROWS)], g.at[1], ld_sem.at[3]),
        pltpu.make_async_copy(b_hbm, w.at[pl.ds(0, R)], ld_sem.at[4]),
        pltpu.make_async_copy(w_hbm, w.at[pl.ds(R, D_LOCAL)], ld_sem.at[5]),
    ]
    for cp in loads:
        cp.start()

    barrier = pltpu.get_barrier_semaphore()
    peers = [(wi, xh * 4 + ring(z, k)) for k in (1, 2, 3)] + [x_cross, partner]
    for dx in (0, 1):
        for k in range(4):
            if dx or k:
                peers.append(wide_dev(xl if dx == 0 else 1 - xl, ring(y, k), c))
    for dev in peers:
        pl.semaphore_signal(barrier, inc=1, device_id=dev, device_id_type=MESH)
    pl.semaphore_wait(barrier, len(peers))

    g_sends = []

    def g_slot(unit, cut):
        slot = unit[0] * 2 + unit[1]
        if cut is None:
            return g.at[slot], slot
        return g.at[slot, pl.ds(*CUTS[cut])], slot if cut == 0 else 16 + unit[0] - 6

    def g_send(src, dst, dev, cut=None):
        ref, sem = g_slot(dst, cut)
        if isinstance(src, tuple):
            src = g_slot(src, cut)[0]
        elif cut is not None:
            src = src.at[pl.ds(*CUTS[cut])]
        send(src, ref, g_ss.at[len(g_sends)], g_rs.at[sem], dev)
        g_sends.append(cut)

    def g_wait(step, kind, cut=None):
        ref, sem = g_slot((step, kind), cut)
        arrived(ref, g_rs.at[sem], g_ss.at[0])

    own0, own1 = g_hbm.at[pl.ds(0, ROWS)], g_hbm.at[pl.ds(ROWS, ROWS)]
    g_send(own0, (2, 0), x_cross)
    g_send(own1, (1, 1), z_next)
    g_send(own0, (1, 0), z_prev)

    def spread_own(buf, ss, rs):
        me = buf.at[wi]
        send(me, me, ss.at[0], rs.at[wi], x_pair)
        for k in (1, 3, 2):
            send(me, me, ss.at[k], rs.at[wi], wide_dev(xl, ring(y, k), c))
        send(me, me, ss.at[4], rs.at[wi], partner)

    def spread_pair(buf, ss, rs, near=True, far=True):
        other = wide_id(1 - xl, y, c)
        blk = buf.at[other]
        if near:
            arrived(blk, rs.at[other], ss.at[0])
            send(blk, blk, ss.at[8], rs.at[other], partner)
        for i, k in enumerate((1, 3, 2)):
            if near and k != 2 or far and k == 2:
                send(blk, blk, ss.at[5 + i], rs.at[other], wide_dev(xl, ring(y, k), c))

    def spread_core(buf, ss, rs, blocks=range(6)):
        for i in blocks:
            other = wide_id(xl if i < 3 else 1 - xl, ring(y, (1, 3, 2)[i % 3]), c)
            blk = buf.at[other]
            arrived(blk, rs.at[other], ss.at[0])
            send(blk, blk, ss.at[9 + i], rs.at[other], partner)

    def spread_end(buf, ss, rs):
        for xl_ in (0, 1):
            for y_ in range(4):
                other = wide_id(xl_, y_, 1 - c)
                arrived(buf.at[other], rs.at[other], ss.at[0])

    loads[0].wait()
    spread_own(xs_all, in_ss, in_rs)

    loads[1].wait()
    low = dot_nn(xs_all[wi], a[...])
    for rh in (0, 1):
        for ch in (0, 1):
            lp[rh * 2 + ch] = low[rh * 56:rh * 56 + 56, ch * 128:ch * 128 + 128]

    def low_stage1():
        for k in (1, 3, 2):
            q = ring(z, k)
            send(lp.at[q], l1.at[3 - k], l1_ss.at[k - 1], l1_rs.at[3 - k], (wi, xh * 4 + q))

    def low_stage2():
        for k in range(3):
            arrived(l1.at[k], l1_rs.at[k], l1_ss.at[k])
        l2s[...] = lp[z] + l1[0] + l1[1] + l1[2]
        send(l2s, l2r, l2_ss, l2_rs, x_cross)

    def low_stage3():
        arrived(l2r, l2_rs, l2_ss)
        lo[z] = l2s[...] + l2r[...]
        for k in (1, 3, 2):
            send(lo.at[z], lo.at[z], l3_ss.at[k - 1], l3_rs.at[z], (wi, xh * 4 + ring(z, k)))

    def low_stage4():
        for k in (1, 2, 3):
            q = ring(z, k)
            arrived(lo.at[q], l3_rs.at[q], l3_ss.at[k - 1])
        top = jnp.concatenate([lo[0], lo[1]], axis=1)
        bottom = jnp.concatenate([lo[2], lo[3]], axis=1)
        la[wi] = jnp.concatenate([top, bottom], axis=0).astype(BF16)
        spread_own(la, la_ss, la_rs)

    low_stage1()
    g_send(own0, (3, 0), z_next)
    g_send(own1, (2, 1), z_prev)

    for cp in loads[2:]:
        cp.wait()

    def owner(step):
        flip, dz = (
            pick(step, [t[i] for t in ORDER[0]]) * (1 - c) + pick(step, [t[i] for t in ORDER[1]]) * c
            for i in (0, 1)
        )
        return (xh + flip) % 2, ring(z, dz)

    def send_part(step, part):
        send(part_send.at[step, part], part_recv.at[step, part],
             c_ss.at[step, part], c_rs.at[step, part], partner)

    def join_cores(step, part):
        xl_n, y_n = owner(step)
        d = (y - y_n + 4) % 4
        arrived(part_recv.at[step, part], c_rs.at[step, part], c_ss.at[step, part])

        def total(h, i):
            return mine[step % 4, part, h, i] + part_recv[step, part, h, i].astype(F32)

        @pl.when(d == 0)
        def _():
            for h in (0, 1):
                for i in range(PER_PART):
                    y_own[xl_n, part, h, i] = total(h, i)

        @pl.when(d == 2)
        def _():
            for h in (0, 1):
                for i in range(PER_PART):
                    part_recv[step, part, h, i] = total(h, i).astype(BF16)
            for h, k in ((0, 3), (1, 1)):
                send(part_recv.at[step, part, h], relay.at[h, xl_n, part], y_ss.at[step, part, h],
                     f_rs.at[h, xl_n, part], wide_dev(xl, ring(y, k), c))

        @pl.when(d % 2 == 1)
        def _():
            late = d // 2
            for i in range(PER_PART):
                mine[step % 4, part, late, i] = total(late, i)
                part_recv[step, part, 1 - late, i] = total(1 - late, i).astype(BF16)
            send(part_recv.at[step, part, 1 - late], y_recv.at[late, xl_n, part, 1 - late],
                 y_ss.at[step, part, 1 - late], y_rs.at[late, xl_n, part, 1 - late], wide_dev(xl, y_n, c))

    def pass_on(step, part):
        xl_n, y_n = owner(step)
        d = (y - y_n + 4) % 4

        @pl.when(d % 2 == 1)
        def _():
            late = d // 2
            arrived(relay.at[late, xl_n, part], f_rs.at[late, xl_n, part], x_ss.at[part])
            for i in range(PER_PART):
                part_recv[step, part, late, i] = (
                    mine[step % 4, part, late, i] + relay[late, xl_n, part, i].astype(F32)
                ).astype(BF16)
            send(part_recv.at[step, part, late], y_recv.at[late, xl_n, part, late],
                 y_ss.at[step, part, late], y_rs.at[late, xl_n, part, late], wide_dev(xl, y_n, c))

    def join_y(step, part):
        xl_n, y_n = owner(step)

        @pl.when(y_n == y)
        def _():
            for r in (0, 1):
                for h in (0, 1):
                    arrived(y_recv.at[r, xl_n, part, h], y_rs.at[r, xl_n, part, h], x_ss.at[part])

            def total(h, i):
                return (y_own[xl_n, part, h, i] + y_recv[0, xl_n, part, h, i].astype(F32)
                        + y_recv[1, xl_n, part, h, i].astype(F32))

            @pl.when(xl_n == xl)
            def _():
                for h in (0, 1):
                    for i in range(PER_PART):
                        y_own[xl_n, part, h, i] = total(h, i)

            @pl.when(xl_n != xl)
            def _():
                for h in (0, 1):
                    for i in range(PER_PART):
                        x_send[part, h, i] = total(h, i).astype(BF16)
                send(x_send.at[part], x_recv.at[part], x_ss.at[part], x_rs.at[part], x_pair)

    def over_parts(do, step):
        def body(part, carry):
            do(step, part)
            return carry

        return lax.fori_loop(0, PARTS, body, 0)

    def pass_on_all(step):
        return over_parts(pass_on, step)

    def join_y_all(step):
        return over_parts(join_y, step)

    def own_total(part, h, i):
        return y_own[xl, part, h, i] + x_recv[part, h, i].astype(F32)

    def announce_all(step):
        xl_n, y_n = owner(step)

        @pl.when((xl_n == xl) & (y_n == y))
        def _():
            arrived(x_recv.at[0], x_rs.at[0], x_ss.at[0])
            lg[wi] = jnp.concatenate([own_total(0, 0, 0), own_total(0, 1, 0)], axis=1).astype(BF16)
            me = lg.at[wi]
            send(me, me, lg_ss.at[0], lg_rs.at[wi], partner)
            for i, (dx, k) in enumerate(CHIPS):
                send(me, me, lg_ss.at[1 + i], lg_rs.at[wi], wide_dev((xl + dx) % 2, ring(y, k), c))

        return 0

    def drain(step, carry):
        xl_n, y_n = owner(step)
        for part in range(PARTS):
            sent(part_send.at[step, part], c_ss.at[step, part], c_rs.at[step, part])

        @pl.when(y_n != y)
        def _():
            for part in range(PARTS):
                for h in (0, 1):
                    sent(part_recv.at[step, part, h], y_ss.at[step, part, h], y_rs.at[0, 0, part, h])

        return carry

    def drain_first():
        for sem in range(5):
            sent(g.at[0], g_ss.at[sem], g_rs.at[0])
        for k in range(3):
            sent(lp.at[0], l1_ss.at[k], l1_rs.at[k])
            sent(lo.at[0], l3_ss.at[k], l3_rs.at[k])
        sent(l2s, l2_ss, l2_rs)
        for i in range(5):
            sent(xs_all.at[wi], in_ss.at[i], in_rs.at[wi])
        lax.fori_loop(0, 2, drain, 0)

    def drain_most():
        for sem, cut in enumerate(g_sends):
            if sem >= 5:
                sent(g.at[0] if cut is None else g.at[0, pl.ds(*CUTS[cut])], g_ss.at[sem], g_rs.at[0])
        for i in range(15):
            sent(la.at[wi], la_ss.at[i], la_rs.at[wi])
            if i >= 5:
                sent(xs_all.at[wi], in_ss.at[i], in_rs.at[wi])
        lax.fori_loop(2, 6, drain, 0)

    def before(step):
        if step == 1:
            g_wait(1, 0)
            low_stage2()
            g_send(g_hbm.at[pl.ds(ROWS, ROWS)], (3, 1), x_cross)
            g_send((1, 0), (6, 0), x_cross)
            g_wait(1, 1)
            g_send(g.at[3], (6, 1), x_cross, 0)
            g_send(g.at[3], (6, 1), x_cross, 1)
        if step == 2:
            g_wait(2, 0)
            g_send((2, 0), (4, 0), z_next)
            low_stage3()
            g_wait(2, 1)
            g_send((2, 1), (4, 1), z_prev)
            g_wait(3, 0)
            g_send((3, 0), (5, 0), z_next)
            spread_pair(xs_all, in_ss, in_rs, far=False)
        if step == 3:
            g_wait(3, 1)
            g_send((3, 1), (5, 1), z_prev)
            spread_pair(xs_all, in_ss, in_rs, near=False)
        if step == 4:
            g_wait(4, 1)
            g_wait(4, 0)
            low_stage4()
        if step == 5:
            g_wait(6, 0)
            g_send((6, 0), (7, 0), z_prev)
            spread_core(xs_all, in_ss, in_rs, range(3))
            join_y_all(0)
            join_y_all(1)
            drain_first()
            g_wait(6, 1, 0)
            g_send((6, 1), (7, 1), z_next, 0)
            g_wait(5, 0)
            g_wait(5, 1)
        if step == 6:
            spread_core(xs_all, in_ss, in_rs, range(3, 6))
            g_wait(6, 1, 1)
            g_send((6, 1), (7, 1), z_next, 1)
            spread_pair(la, la_ss, la_rs)
        if step == 7:
            spread_core(la, la_ss, la_rs)
            g_wait(7, 0)
            g_wait(7, 1, 0)
            g_wait(7, 1, 1)

    def step_body(step, carry):
        for k in range(1, STEPS):
            @pl.when(step == k)
            def _(k=k):
                before(k)

        def tile_body(t, carry):
            rows = g[pl.ds(step * 2, 2)].reshape(2 * ROWS, F_LOCAL)
            cols = w[pl.ds(pl.multiple_of(t * TILE, TILE), TILE), :]
            acc = dot_nt(rows, cols)
            top, bottom = acc[:ROWS], acc[ROWS:]
            keep, give = jnp.where(c == 0, top, bottom), jnp.where(c == 0, bottom, top).astype(BF16)
            part, i = t // PER_PART, t % PER_PART
            for h in (0, 1):
                mine[step % 4, part, h, i] = keep[:, h * HALF:h * HALF + HALF]
                part_send[step, part, h, i] = give[:, h * HALF:h * HALF + HALF]

            @pl.when(t == 4 + 3 * (step >= 6).astype(jnp.int32))
            def _():
                lax.fori_loop(pick(step, PASSED), pick(step, PASSED[1:]), lambda s, carry: pass_on_all(s), 0)

            @pl.when((t == 8) & (step >= 6))
            def _():
                lax.fori_loop(pick(step, JOINED), pick(step, JOINED[1:]), lambda s, carry: join_y_all(s), 0)

            @pl.when(t == 3)
            def _():
                send_part(step, 0)

            @pl.when((t == 5) | (t == 8))
            def _():
                join_cores(step, t // 4 - 1)

            @pl.when(t == 6)
            def _():
                send_part(step, 1)

            return carry

        lax.fori_loop(0, TILES, tile_body, 0)
        send_part(step, 2)
        join_cores(step, 2)

        return carry

    lax.fori_loop(0, STEPS, step_body, 0)
    pass_on_all(7)
    join_y_all(6)
    lax.fori_loop(0, 6, lambda s, carry: announce_all(s), 0)

    scale = ADAPTER_SCALE / (16 * ROWS)

    spread_end(la, la_ss, la_rs)
    for s in range(STEPS):
        for kind in (0, 1):
            flip, dz = ORDER[kind][s]
            n = ((xh + flip) % 2) * 4 + ring(z, dz)
            la_t[pl.ds((s * 2 + kind) * ROWS, ROWS), :] = la[n * 2 + kind]
    lg_t[...] = la_t[...].T

    def gb_body(t, carry):
        cols = pl.ds(pl.multiple_of(t * TILE, TILE), TILE)
        tokens = g[:, :, cols].reshape(16 * ROWS, TILE)
        gb_ref[:, cols] = scale * dot_nn(lg_t[...], tokens)
        return carry

    lax.fori_loop(0, F_LOCAL // TILE, gb_body, 0)
    gb_out = pltpu.make_async_copy(gb_ref, gb_hbm, out_sem.at[0])
    gb_out.start()

    announce_all(6)
    drain_most()
    join_y(7, 0)
    announce_all(7)
    join_y(7, 1)
    join_y(7, 2)
    for i, (dx, k) in enumerate(CHIPS):
        other = wide_id((xl + dx) % 2, ring(y, k), c)
        blk = lg.at[other]
        arrived(blk, lg_rs.at[other], lg_ss.at[0])
        send(blk, blk, lg_ss.at[8 + i], lg_rs.at[other], partner)

    low_rows = lg[wi]

    def ig_body(t, carry):
        cols = pl.ds(pl.multiple_of(t * TILE, TILE), TILE)
        part, i = (t + 1) // PER_PART, (t + 1) % PER_PART
        base = jnp.concatenate([own_total(part, 0, i), own_total(part, 1, i)], axis=1)
        ig_ref[t] = (base + ADAPTER_SCALE * dot_nt(low_rows, a[cols, :])).astype(BF16)
        pltpu.make_async_copy(ig_ref.at[t], ig_hbm.at[:, cols], ig_sem.at[t]).start()
        return carry

    def ig_part(part):
        if part:
            arrived(x_recv.at[part], x_rs.at[part], x_ss.at[part])
        lax.fori_loop(max(part * PER_PART - 1, 0), (part + 1) * PER_PART - 1, ig_body, 0)

    ig_part(0)
    ig_part(1)

    spread_end(xs_all, in_ss, in_rs)
    spread_end(lg, lg_ss, lg_rs)
    lg_t[...] = lg[...].reshape(16 * ROWS, R).T

    def ga_body(t, carry):
        cols = pl.ds(pl.multiple_of(t * TILE, TILE), TILE)
        tokens = xs_all[:, :, cols].reshape(16 * ROWS, TILE)
        ga_ref[t] = scale * dot_nn(lg_t[...], tokens)
        pltpu.make_async_copy(ga_ref.at[t], ga_hbm.at[t], out_sem.at[2 + t]).start()
        return carry

    lax.fori_loop(0, D_LOCAL // TILE, ga_body, 0)

    ig_part(2)
    for i in range(15):
        sent(lg.at[wi], lg_ss.at[i], lg_rs.at[wi])
    lax.fori_loop(6, STEPS, drain, 0)
    gb_out.wait()
    for t in range(D_LOCAL // TILE):
        pltpu.make_async_copy(ga_ref.at[t], ga_hbm.at[t], out_sem.at[2 + t]).wait()
    for t in range(D_LOCAL // TILE):
        cols = pl.ds(t * TILE, TILE)
        pltpu.make_async_copy(ig_ref.at[t], ig_hbm.at[:, cols], ig_sem.at[t]).wait()
    for part in range(PARTS):
        sent(x_send.at[part], x_ss.at[part], x_rs.at[part])


def results(ig, ga, gb, ig_out, ga_out, gb_out, ig_buf, ga_buf, gat_buf, gb_buf, in_sem, out_sem):
    blocks = D_LOCAL // TILE
    rows = R // 4
    pairs = [(ga.at[t], ga_buf.at[t], gat_buf.at[t], ga_out.at[pl.ds(t * TILE, TILE)]) for t in range(blocks)]
    for i in range(4):
        cut = pl.ds(i * rows, rows)
        pairs.append((gb.at[cut], gb_buf.at[cut], gb_buf.at[cut], gb_out.at[cut]))
    pairs.append((ig, ig_buf, ig_buf, ig_out))
    loads = [pltpu.make_async_copy(p[0], p[1], in_sem.at[i]) for i, p in enumerate(pairs)]
    stores = [pltpu.make_async_copy(p[2], p[3], out_sem.at[i]) for i, p in enumerate(pairs)]
    for cp in loads:
        cp.start()
    for i in range(len(pairs)):
        loads[i].wait()
        if i < blocks:
            gat_buf[i] = ga_buf[i].T
        stores[i].start()
    for cp in stores:
        cp.wait()


def shards(inputs, grad_out, w_base, adapter_down_matrix, b_factor):
    dma = pltpu.SemaphoreType.DMA
    pieces = (PARTS, 2, PER_PART, ROWS, HALF)
    scratch = [
        pltpu.VMEM((D_LOCAL // TILE, ROWS, TILE), BF16),
        pltpu.VMEM((D_LOCAL // TILE, R, TILE), F32),
        pltpu.VMEM((R, F_LOCAL), F32),
        pltpu.VMEM((16, ROWS, F_LOCAL), BF16),
        pltpu.VMEM((R + D_LOCAL, F_LOCAL), BF16),
        pltpu.VMEM((D_LOCAL, R), BF16),
        pltpu.VMEM((16, ROWS, D_LOCAL), BF16),
        pltpu.VMEM((STEPS,) + pieces, BF16),
        pltpu.VMEM((STEPS,) + pieces, BF16),
        pltpu.VMEM((4,) + pieces, F32),
        pltpu.VMEM((2, 2, PARTS, PER_PART, ROWS, HALF), BF16),
        pltpu.VMEM((2, 2) + pieces, BF16),
        pltpu.VMEM((2,) + pieces, F32),
        pltpu.VMEM(pieces, BF16),
        pltpu.VMEM(pieces, BF16),
        pltpu.VMEM((4, 56, 128), F32),
        pltpu.VMEM((3, 56, 128), F32),
        pltpu.VMEM((56, 128), F32),
        pltpu.VMEM((56, 128), F32),
        pltpu.VMEM((4, 56, 128), F32),
        pltpu.VMEM((16, ROWS, R), BF16),
        pltpu.VMEM((16 * ROWS, R), BF16),
        pltpu.VMEM((16, ROWS, R), BF16),
        pltpu.VMEM((R, 16 * ROWS), BF16),
        dma((6,)), dma((10,)), dma((8,)), dma((16,)), dma((18,)), dma((STEPS, PARTS)), dma((STEPS, PARTS)),
        dma((2, 2, PARTS)), dma((STEPS, PARTS, 2)), dma((2, 2, PARTS, 2)), dma((PARTS,)), dma((PARTS,)),
        dma((15,)), dma((16,)), dma((15,)), dma((16,)), dma((15,)), dma((16,)),
        dma((3,)), dma((3,)), dma(()), dma(()), dma((3,)), dma((4,)),
    ]
    any_spec = pl.BlockSpec(memory_space=pl.ANY)
    input_gradient, grad_a, grad_b = pl.pallas_call(
        kernel,
        out_shape=(
            jax.ShapeDtypeStruct((ROWS, D_LOCAL), BF16),
            jax.ShapeDtypeStruct((D_LOCAL // TILE, R, TILE), F32),
            jax.ShapeDtypeStruct((R, F_LOCAL), F32),
        ),
        in_specs=[any_spec] * 5,
        out_specs=(any_spec,) * 3,
        scratch_shapes=scratch,
        compiler_params=pltpu.CompilerParams(
            collective_id=0, has_side_effects=True, vmem_limit_bytes=67043328
        ),
        name="backward",
    )(inputs, grad_out, w_base, adapter_down_matrix, b_factor)
    blocks = D_LOCAL // TILE
    return pl.pallas_call(
        results,
        out_shape=(
            jax.ShapeDtypeStruct((ROWS, D_LOCAL), BF16),
            jax.ShapeDtypeStruct((D_LOCAL, R), F32),
            jax.ShapeDtypeStruct((R, F_LOCAL), F32),
        ),
        in_specs=[any_spec] * 3,
        out_specs=(any_spec,) * 3,
        scratch_shapes=[
            pltpu.VMEM((ROWS, D_LOCAL), BF16),
            pltpu.VMEM((blocks, R, TILE), F32),
            pltpu.VMEM((blocks, TILE, R), F32),
            pltpu.VMEM((R, F_LOCAL), F32),
            dma((blocks + 5,)),
            dma((blocks + 5,)),
        ],
        name="results",
    )(input_gradient, grad_a, grad_b)


def solution(mesh):
    return jax.shard_map(
        shards,
        mesh=mesh,
        in_specs=(
            P("wide", "narrow"),
            P("narrow", "wide"),
            P("narrow", "wide"),
            P("narrow", None),
            P(None, "wide"),
        ),
        out_specs=(P("wide", "narrow"), P("narrow", None), P(None, "wide")),
        check_vma=False,
    )
```
